512 devices in a mesh: sector: 256 (over z, y, x), chan: 2 (over core).
Axes of the slice: x: 4, y: 8, z: 8, core: 2. Of those that a mesh axis runs over, the one named last changes fastest.
Arguments:
- atm_state: bfloat16 [160, 262144], P('chan', 'sector'), may hold values from -6 to 6
- ocean_state: bfloat16 [160, 262144], P('chan', 'sector'), may hold values from -6 to 6
- wet_mask: int32 [262144], P('sector'), may hold values from 0 to 1, as said below
- neighbours: int32 [8, 262144], P(None, 'sector'), may hold values from 0 to 1087, as said below
- west_rim: int32 [8192], P('sector'), may hold values from 0 to 1023, as said below
- east_rim: int32 [8192], P('sector'), may hold values from 0 to 1023, as said below
- atm_gain: float32 [160], replicated, may hold values from 0.5 to 1.5
- atm_conv_in: bfloat16 [160, 9, 160], P('chan'), may hold values from -0.15625 to 0.15625
- atm_conv_out: bfloat16 [160, 9, 160], P('chan'), may hold values from -0.15625 to 0.15625
- ocean_conv: bfloat16 [160, 9, 160], P('chan'), may hold values from -0.15625 to 0.15625
- ocean_gain: float32 [160], replicated, may hold values from 0.5 to 1.5
- mlp_in: bfloat16 [640, 160], replicated, may hold values from -0.5 to 0.5
- mlp_out: bfloat16 [160, 640], replicated, may hold values from -0.25 to 0.25
Outputs:
- atm_next: bfloat16 [160, 262144], P('chan', 'sector')
- ocean_next: bfloat16 [160, 262144], P('chan', 'sector')
The draws below stay inside these ranges and needn't reach their ends.
Inputs may be any that keep to these rules, and one draw needn't show every extreme that they name: Each sector is a grid of 32 cycles by 32 columns, stored cycle by cycle (32 positions to a cycle, cycle r at positions r * 32 to r * 32 + 31) with the columns in a permuted order within each cycle; a pixel's 8 neighbours are its compass neighbours on that grid, a cycle index beyond the grid's ends taken as the nearest cycle; a column beyond the west end refers to slot 1024 + cycle (the west sector's east rim pixel of that cycle), beyond the east end to slot 1056 + cycle. `west_rim`: the local positions of the sector's westmost column, cycle by cycle, consistent with neighbours. `east_rim`: the local positions of the sector's eastmost column, cycle by cycle, consistent with neighbours. `wet_mask`: the wet pixels of a sector and of the sector half the loop away number exactly 1024 together; some sector is all ocean.
All inputs are finite; a program needn't handle non-finite values.
Results may differ from the reference program's by a relative error of at most 0.013.
Values may be sent and summed in bfloat16 or wider, within the bound.
A program may use at most 64 MiB of HBM per device.

```python
import jax
import jax.numpy as jnp
from jax import lax

C = 160
HID = 640
RW = 32
LW = 32
PIX = 1024
NPIX = 262144
NRIM = 8192
N_SECTOR = 256


COMPASS = ((-1, -1), (-1, 0), (-1, 1), (0, -1), (0, 1), (1, -1), (1, 0), (1, 1))


def sector_layout(key):
    streams = jax.random.split(jax.random.fold_in(key, 5), N_SECTOR * RW)
    shuffled = jax.vmap(lambda stream: jax.random.permutation(stream, LW))(streams).astype(jnp.int32)
    shuffled = shuffled.reshape(N_SECTOR, RW, LW)
    cycle_base = (jnp.arange(RW, dtype=jnp.int32) * LW)[None, :, None]
    return (cycle_base + shuffled).reshape(N_SECTOR, PIX).astype(jnp.int32)


def mask_ranks(key):
    streams = jax.random.split(jax.random.fold_in(key, 7), N_SECTOR)
    return jax.vmap(lambda stream: jax.random.permutation(stream, PIX))(streams).astype(jnp.int32)


def draw_neighbours(key, part):
    layout = sector_layout(key)
    cell_ids = jnp.arange(PIX, dtype=jnp.int32)
    cycle_of = cell_ids // LW
    column = cell_ids % LW

    def one_sector(places):
        tables = []
        for cycle_step, column_step in COMPASS:
            near_cycle = jnp.clip(cycle_of + cycle_step, 0, RW - 1)
            near_column = column + column_step
            inside = (near_column >= 0) & (near_column < LW)
            near_cell = near_cycle * LW + jnp.clip(near_column, 0, LW - 1)
            outside = jnp.where(near_column < 0, PIX + near_cycle, PIX + RW + near_cycle)
            tables.append(jnp.where(inside, places[near_cell], outside).astype(jnp.int32))
        by_cell = jnp.stack(tables)
        return jnp.zeros((8, PIX), jnp.int32).at[:, places].set(by_cell)
    per_sector = jax.vmap(one_sector)(layout)
    return per_sector.transpose(1, 0, 2).reshape(8, NPIX)


def draw_west_rim(key, part):
    layout = sector_layout(key)
    return layout[:, jnp.arange(RW, dtype=jnp.int32) * LW].reshape(NRIM)


def draw_east_rim(key, part):
    layout = sector_layout(key)
    return layout[:, jnp.arange(RW, dtype=jnp.int32) * LW + LW - 1].reshape(NRIM)


def draw_wet_mask(key, part):
    half_count = N_SECTOR // 2
    counts = jax.random.randint(jax.random.fold_in(key, 11), (half_count,), 0, PIX + 1)
    chosen = jax.random.randint(jax.random.fold_in(key, 12), (), 0, half_count)
    counts = jnp.where(jnp.arange(half_count) == chosen, PIX, counts)
    counts = jnp.concatenate([counts, PIX - counts]).astype(jnp.int32)
    ranks = mask_ranks(jax.random.fold_in(key, 13))
    return (ranks < counts[:, None]).astype(jnp.int32).reshape(NPIX)


def block_levels(rng, extent, cuts, least, largest):
    factor_of = 1.0
    for axis_at, shards_of in cuts:
        draws = jax.random.uniform(jax.random.fold_in(jax.random.fold_in(rng, 6), axis_at), (shards_of,), jnp.float32, least / len(cuts), largest / len(cuts))
        factor_of = factor_of * jnp.repeat(jnp.exp(draws), extent[axis_at] // shards_of).reshape((-1,) + (1,) * (len(extent) - 1 - axis_at))
    return factor_of


def noise(stream_key, shape, scale, bound, cuts=(), kind=jnp.bfloat16):
    result = jax.random.normal(stream_key, shape, jnp.float32) * scale
    if len(cuts) > 0:
        result = block_levels(stream_key, shape, cuts, -0.22, 0.18) * result
    return jnp.clip(result, min=-bound, max=bound).astype(kind)


def setup_inputs(seed: int = 0) -> dict:
    splits = jax.random.split(jax.random.key(seed), 14)
    atm_state = noise(splits[0], (C, NPIX), 1.0, 6.0, ((0, 2), (1, 256)))
    ocean_state = noise(splits[1], (C, NPIX), 1.0, 6.0, ((0, 2), (1, 256)))
    wet_mask = draw_wet_mask(jax.random.fold_in(splits[13], 71), 0)
    neighbours = draw_neighbours(jax.random.fold_in(splits[13], 71), 0)
    west_rim = draw_west_rim(jax.random.fold_in(splits[13], 71), 0)
    east_rim = draw_east_rim(jax.random.fold_in(splits[13], 71), 0)
    atm_gain = jnp.clip(jax.random.uniform(splits[6], (C,), jnp.float32, 0.5, 1.5), 0.5, 1.5)
    atm_conv_in = noise(splits[7], (C, 9, C), (9 * C) ** -0.5, 0.15625, ((0, 2),))
    atm_conv_out = noise(splits[8], (C, 9, C), (9 * C) ** -0.5, 0.15625, ((0, 2),))
    ocean_conv = noise(splits[9], (C, 9, C), (9 * C) ** -0.5, 0.15625, ((0, 2),))
    ocean_gain = jnp.clip(jax.random.uniform(splits[10], (C,), jnp.float32, 0.5, 1.5), 0.5, 1.5)
    mlp_in = noise(splits[11], (HID, C), C ** -0.5, 0.5)
    mlp_out = noise(splits[12], (C, HID), HID ** -0.5, 0.25)
    return {"atm_state": atm_state, "ocean_state": ocean_state, "wet_mask": wet_mask, "neighbours": neighbours, "west_rim": west_rim, "east_rim": east_rim, "atm_gain": atm_gain, "atm_conv_in": atm_conv_in, "atm_conv_out": atm_conv_out, "ocean_conv": ocean_conv, "ocean_gain": ocean_gain, "mlp_in": mlp_in, "mlp_out": mlp_out}


EPSILON = 1e-06

def normalize(values_in, scales):
    values = values_in.astype(jnp.float32)
    mean_sq = lax.optimization_barrier(jnp.mean(values * values, axis=0, keepdims=True))
    return (values * lax.rsqrt(mean_sq + EPSILON) * scales[:, None]).astype(jnp.bfloat16)

def global_sources(neighbours, west_rim, east_rim):
    column = jnp.arange(NPIX, dtype=jnp.int32)
    sector = column // PIX
    before = (sector + N_SECTOR - 1) % N_SECTOR
    following = (sector + 1) % N_SECTOR
    west_slot = jnp.clip(neighbours - PIX, 0, RW - 1)
    east_slot = jnp.clip(neighbours - PIX - RW, 0, RW - 1)
    from_west = before * PIX + east_rim[before * RW + west_slot]
    from_east = following * PIX + west_rim[following * RW + east_slot]
    inside = sector * PIX + jnp.clip(neighbours, 0, PIX - 1)
    chosen = jnp.where(neighbours < PIX, inside, jnp.where(neighbours < PIX + RW, from_west, from_east))
    return chosen.astype(jnp.int32)

def convolve(values_in, weight, sources):
    running = jnp.dot(weight[:, 0, :], values_in, preferred_element_type=jnp.float32)
    for neighbour in range(8):
        moved = jnp.take(values_in, sources[neighbour], axis=1)
        running = running + jnp.dot(weight[:, neighbour + 1, :], moved, preferred_element_type=jnp.float32)
    return running

def atmos_step(current, scales, w_first, w_second, sources):
    normed = normalize(current, scales)
    hidden = jax.nn.gelu(convolve(normed, w_first, sources), approximate=True).astype(jnp.bfloat16)
    return (current.astype(jnp.float32) + convolve(hidden, w_second, sources)).astype(jnp.bfloat16)

def reference(atm_state, ocean_state, wet_mask, neighbours, west_rim, east_rim, atm_gain, atm_conv_in, atm_conv_out, ocean_conv, ocean_gain, mlp_in, mlp_out):
    sources = global_sources(neighbours, west_rim, east_rim)
    state_one = atmos_step(atm_state, atm_gain, atm_conv_in, atm_conv_out, sources)
    state_two = atmos_step(state_one, atm_gain, atm_conv_in, atm_conv_out, sources)
    wet_rows = wet_mask.astype(jnp.float32)[None, :]
    forcing = ((ocean_state.astype(jnp.float32) + 0.5 * (state_one.astype(jnp.float32) + state_two.astype(jnp.float32))) * wet_rows).astype(jnp.bfloat16)
    mixed_rows = convolve(forcing, ocean_conv, sources).astype(jnp.bfloat16)
    blocks = mixed_rows.reshape(C, N_SECTOR, PIX).transpose(1, 0, 2)

    def column_set(part_rows):
        normed = normalize(part_rows, ocean_gain)
        hidden = jax.nn.gelu(jnp.dot(mlp_in, normed, preferred_element_type=jnp.float32), approximate=True).astype(jnp.bfloat16)
        return jnp.dot(mlp_out, hidden, preferred_element_type=jnp.float32).astype(jnp.bfloat16)
    update = lax.map(column_set, blocks).transpose(1, 0, 2).reshape(C, NPIX)
    ocean_next = (ocean_state.astype(jnp.float32) + wet_rows * update.astype(jnp.float32)).astype(jnp.bfloat16)
    return (state_two, ocean_next)
```

```python
import functools

import jax
import jax.numpy as jnp
from jax import lax
from jax.experimental import pallas as pl
from jax.experimental.pallas import tpu as pltpu
from jax.sharding import PartitionSpec as P

EPSILON = 1e-06
CH = 80
C = 160
ROWS = 32
STRIDE = 48
BUF = 1104
MESH = pl.DeviceIdType.MESH
NT = (((1,), (1,)), ((), ()))
TN = (((0,), (0,)), ((), ()))
F32 = jnp.float32
BF = jnp.bfloat16


def iota(shape, dim):
    return lax.broadcasted_iota(jnp.int32, shape, dim)


def onehot(hit):
    return jnp.where(hit, 1.0, 0.0).astype(BF)


def tap_slot(dyi, dxi):
    m = 3 * dyi + dxi
    return 0 if m == 4 else (m + 1 if m < 4 else m)


def kernel(
    nb, wet, ga, go, atm, oc, w1, w2, w3, mi, mo,
    out_a, out_o,
    xa, xo, wraw, wb, miv, mov, keys, tsel, sbuf, halo, st_a, st_b, oc_a, oc_b,
    va, vb, bc, pbuf, nrm, fin, obuf, nbv,
    lsem, psem_s, psem_r, hsem_s, hsem_r, osem_s, osem_r,
):
    sectors = lax.axis_size("sector")
    s = lax.axis_index("sector")
    c = lax.axis_index("chan")
    pc = 1 - c
    west = lax.rem(s + sectors - 1, sectors)
    east = lax.rem(s + 1, sectors)
    partner = {"sector": s, "chan": pc}

    bar = pltpu.get_barrier_semaphore()
    pl.semaphore_signal(bar, inc=1, device_id=partner, device_id_type=MESH)
    for chip in (west, east):
        for t in range(2):
            pl.semaphore_signal(
                bar, inc=1, device_id={"sector": chip, "chan": t}, device_id_type=MESH
            )

    loads = [
        pltpu.make_async_copy(nb, nbv, lsem.at[0]),
        pltpu.make_async_copy(atm, xa.at[c], lsem.at[1]),
        pltpu.make_async_copy(oc, xo.at[c], lsem.at[2]),
        pltpu.make_async_copy(w1, wraw.at[0, c], lsem.at[3]),
        pltpu.make_async_copy(w2, wraw.at[1, c], lsem.at[4]),
        pltpu.make_async_copy(w3, wraw.at[2, c], lsem.at[5]),
        pltpu.make_async_copy(mi, miv, lsem.at[6]),
        pltpu.make_async_copy(mo, mov, lsem.at[7]),
    ]
    for load in loads:
        load.start()
    loads[0].wait()

    for b in range(8):
        lane = iota((8, 128), 1)
        v = jnp.broadcast_to(nbv[3:4, 128 * b : 128 * b + 128], (8, 128))
        inside = v < 1024
        hop = jnp.where(inside, v - 128 * b, lane)
        col = jnp.where(inside, 1, 0)
        for _ in range(5):
            col = col + jnp.take_along_axis(col, hop, axis=1, mode="promise_in_bounds")
            hop = jnp.take_along_axis(hop, hop, axis=1, mode="promise_in_bounds")
        cyc = 4 * b + lax.shift_right_logical(lane, 5)
        keys[0, :, 128 * b : 128 * b + 128] = 32 * cyc + col
        keys[1, :, 128 * b : 128 * b + 128] = 32 * (31 - cyc) + col

    loads[1].wait()
    loads[2].wait()

    wet16 = jnp.broadcast_to(wet[...], (16, 1024)).astype(F32).astype(BF)

    hr = iota((256, 256), 0)
    hh = hr & 127
    far = hr >= 128
    hi = lax.shift_right_logical(hh * 205, 10)
    he = hh - 5 * hi
    key_a = jnp.where(hh < 105, 32 * hi + jnp.where(far, 27 + he, he), -1)
    key_o = jnp.where(
        (hh >= 105) & (hh < 122), 32 * (hh - 105) + jnp.where(far, 31, 0), -1
    )
    z16 = jnp.zeros((16, 256), BF)
    for t in range(2):
        total = jnp.zeros((96, 256), F32)
        for b in range(3):
            q = 256 * (b if t == 0 else 3 - b)
            key_q = keys[t, 0:1, q : q + 256]
            x_a = jnp.concatenate([xa[c, :, q : q + 256], z16], axis=0)
            x_o = jnp.concatenate([xo[c, :, q : q + 256], wet16[:, q : q + 256]], axis=0)
            total = total + lax.dot_general(
                x_a, onehot(key_a == key_q), NT, preferred_element_type=F32
            )
            total = total + lax.dot_general(
                x_o, onehot(key_o == key_q), NT, preferred_element_type=F32
            )
        sbuf[t, 0] = total[:, :128].astype(BF)
        sbuf[t, 1] = total[:, 128:].astype(BF)

    pl.semaphore_wait(bar, 5)

    halo_copies = []
    for t in range(2):
        for d, chip in ((0, west), (1, east)):
            halo_copies.append(
                pltpu.make_async_remote_copy(
                    src_ref=sbuf.at[t, d],
                    dst_ref=halo.at[c, :, pl.ds(128 * d, 128)],
                    send_sem=hsem_s.at[2 * t + d],
                    recv_sem=hsem_r.at[d, c],
                    device_id={"sector": chip, "chan": t},
                    device_id_type=MESH,
                )
            )
    for copy in halo_copies:
        copy.start()

    def to_partner(src, dst, n):
        return pltpu.make_async_remote_copy(
            src_ref=src,
            dst_ref=dst,
            send_sem=psem_s.at[n],
            recv_sem=psem_r.at[n],
            device_id=partner,
            device_id_type=MESH,
        )

    window = pl.ds(pl.multiple_of(256 * pc, 256), 768)
    pair = [
        to_partner(atm.at[:, window], xa.at[c, :, window], 0),
        to_partner(w1, wraw.at[0, c], 1),
        to_partner(oc.at[:, window], xo.at[c, :, window], 2),
        to_partner(w2, wraw.at[1, c], 3),
        to_partner(w3, wraw.at[2, c], 4),
    ]
    for copy in pair:
        copy.start()

    for b in range(3):
        q = pl.multiple_of(256 * jnp.where(c == 0, b, 3 - b), 256)
        key_q = keys[c, 0:1, pl.ds(q, 256)] - 256 * b
        tsel[b] = onehot(iota((256, 256), 0) == key_q)

    def prepare(n):
        wb[n, :, 480:512] = jnp.zeros((512, 32), BF)
        wb[n, 480:512, :] = jnp.zeros((32, 512), BF)
        for dyi in range(3):
            for dxi in range(3):
                k = jnp.where(c == 0, tap_slot(dyi, dxi), tap_slot(2 - dyi, dxi))
                w_0 = wraw[n, 0, k]
                w_1 = wraw[n, 1, k]
                for lanes, dst, width in (
                    (slice(0, 128), 128 * dyi, 128),
                    (slice(128, 160), 384 + 32 * dyi, 32),
                ):
                    r = 128 * dxi
                    wb[n, r : r + 80, dst : dst + width] = w_0[:, lanes]
                    wb[n, r + 80 : r + 128, dst : dst + width] = w_1[0:48, lanes]
                    r = 384 + 32 * dxi
                    wb[n, r : r + 32, dst : dst + width] = w_1[48:80, lanes]

    loads[3].wait()
    pair[1].wait_recv()
    prepare(0)

    gain_a = ga[:, 0:128]
    gain_b = jnp.concatenate([ga[:, 128:160], jnp.zeros((1, 96), F32)], axis=1)
    ocean_a = go[:, 0:128]
    ocean_b = jnp.concatenate([go[:, 128:160], jnp.zeros((1, 96), F32)], axis=1)

    pair[0].wait_recv()
    pair[2].wait_recv()
    for b in range(3):
        q = pl.multiple_of(256 * jnp.where(c == 0, b, 3 - b), 256)
        x_a = jnp.concatenate(
            [xa[0, :, pl.ds(q, 256)], xa[1, :, pl.ds(q, 256)], jnp.zeros((96, 256), BF)], axis=0
        )
        wet_b = jnp.broadcast_to(wet[:, pl.ds(q, 256)], (16, 256)).astype(F32).astype(BF)
        x_o = jnp.concatenate(
            [xo[0, :, pl.ds(q, 256)], xo[1, :, pl.ds(q, 256)], wet_b, jnp.zeros((80, 256), BF)],
            axis=0,
        )
        v_a = lax.dot_general(tsel[b], x_a, NT, preferred_element_type=F32)
        v_o = lax.dot_general(tsel[b], x_o, NT, preferred_element_type=F32)
        for il in range(8):
            i = 8 * b + il
            rows = slice(32 * il, 32 * il + 32)
            for g in [STRIDE * (i + 1) + 16] + ([16] if i == 0 else []):
                if i <= 20:
                    st_a[g : g + 32] = v_a[rows, :128]
                    st_b[g : g + 32] = v_a[rows, 128:]
                if i <= 16:
                    oc_a[g : g + 32] = v_o[rows, :128]
                    oc_b[g : g + 32] = v_o[rows, 128:]

    for d in range(2):
        for sender in range(2):
            pltpu.make_async_remote_copy(
                src_ref=sbuf.at[0, d],
                dst_ref=halo.at[sender, :, pl.ds(128 * d, 128)],
                send_sem=hsem_s.at[0],
                recv_sem=hsem_r.at[d, sender],
                device_id=partner,
                device_id_type=MESH,
            ).wait_recv()
    h_all = jnp.concatenate(
        [halo[0, 0:80], halo[1, 0:80], halo[0, 80:96], jnp.zeros((80, 256), BF)], axis=0
    )
    hl = iota((1, 256), 1)
    hh = hl & 127
    far = hl >= 128
    hi = lax.shift_right_logical(hh * 205, 10)
    he = hh - 5 * hi
    p1 = jnp.where(hh < 105, jnp.where(far, 16 * hi + 27 + he, 16 * hi + 32 + he), -1)
    p2 = jnp.where(hi == 0, p1 - 16, p1)
    r = iota((368, 256), 0)
    v_a = lax.dot_general(
        onehot((r == p1) | (r == p2)), h_all, NT, preferred_element_type=F32
    )
    oi = hh - 105
    p1 = jnp.where(
        (oi >= 0) & (oi < 17), jnp.where(far, 16 * oi + 31, 16 * oi + 32), -1
    )
    p2 = jnp.where(oi == 0, p1 - 16, p1)
    r = iota((304, 256), 0)
    v_o = lax.dot_general(
        onehot((r == p1) | (r == p2)), h_all, NT, preferred_element_type=F32
    )
    for k in range(23):
        rows = slice(16 * k, 16 * k + 16)
        g = STRIDE * k
        st_a[g : g + 16] = v_a[rows, :128]
        st_b[g : g + 16] = v_a[rows, 128:]
        if k < 19:
            oc_a[g : g + 16] = v_o[rows, :128]
            oc_b[g : g + 16] = v_o[rows, 128:]

    low = iota((STRIDE, 128), 1) < 32

    def normed(x_a, x_b, scale_a, scale_b):
        x_b = jnp.where(low, x_b, 0.0)
        mean_sq = jnp.sum(x_a * x_a + x_b * x_b, axis=1, keepdims=True) * (1.0 / C)
        inv = lax.rsqrt(mean_sq + EPSILON)
        return x_a * inv * scale_a, x_b * inv * scale_b

    def put(g, x_a, x_b):
        va[pl.ds(g, STRIDE)] = x_a.astype(BF)
        vb[pl.ds(g, STRIDE)] = jnp.where(low, x_b, 0.0).astype(BF).astype(F32)

    @pl.loop(0, 22)
    def _(m):
        g = pl.multiple_of(STRIDE * m, STRIDE)
        x_a, x_b = normed(
            st_a[pl.ds(g, STRIDE)], st_b[pl.ds(g, STRIDE)], gain_a, gain_b
        )
        put(g, x_a, x_b)

    top = slice(1056, 1072)
    x_a, x_b = st_a[top], st_b[top]
    mean_sq = jnp.sum(x_a * x_a + x_b * x_b, axis=1, keepdims=True) * (1.0 / C)
    inv = lax.rsqrt(mean_sq + EPSILON)
    va[top] = (x_a * inv * gain_a).astype(BF)
    vb[top] = (x_b * inv * gain_b).astype(BF).astype(F32)

    def convolve(n, wi, epilogue):
        size = 16 + STRIDE * n

        @pl.loop(0, n + 1)
        def _(m):
            g = pl.multiple_of(STRIDE * m + STRIDE, STRIDE)
            bc[pl.ds(g, STRIDE)] = (
                vb[pl.ds(g - STRIDE, STRIDE)]
                + pltpu.roll(vb[pl.ds(g, STRIDE)], 32, 1)
                + pltpu.roll(vb[pl.ds(g + STRIDE, STRIDE)], 64, 1)
            ).astype(BF)

        lhs = jnp.concatenate(
            [va[0:size], va[48 : 48 + size], va[96 : 96 + size], bc[48 : 48 + size]], axis=1
        )
        pbuf[48 : 48 + size] = lax.dot_general(lhs, wb[wi], NT, preferred_element_type=F32)

        @pl.loop(0, n + 1)
        def _(m):
            g = pl.multiple_of(STRIDE * m + STRIDE, STRIDE)
            x = pbuf[pl.ds(g - 8, STRIDE + 16)]
            mid = slice(8, 8 + STRIDE)
            p_b = x[:, 384:512]
            out_a = (
                x[mid, 128:256]
                + pltpu.roll(x[:, 0:128], 1, 0)[mid]
                + pltpu.roll(x[:, 256:384], STRIDE + 15, 0)[mid]
            )
            out_b = (
                pltpu.roll(p_b, 1, 0)[mid]
                + pltpu.roll(p_b[mid], 96, 1)
                + pltpu.roll(pltpu.roll(p_b, STRIDE + 15, 0)[mid], 64, 1)
            )
            epilogue(m, g, out_a, out_b)

    def replicate():
        first = iota((16, 128), 0) < 8
        for ref in (va, vb):
            own, nxt = ref[48:64], ref[96:112]
            ref[0:16] = own
            ref[16:48] = ref[64:96]
            ref[48:64] = jnp.where(first, nxt.astype(F32), own.astype(F32)).astype(ref.dtype)

    def gelu(x):
        return jax.nn.gelu(x, approximate=True)

    def hidden(m, g, o_a, o_b):
        put(g, gelu(o_a), gelu(o_b))

    def first_state(m, g, o_a, o_b):
        s_a = (st_a[pl.ds(g, STRIDE)] + o_a).astype(BF).astype(F32)
        s_b = (st_b[pl.ds(g, STRIDE)] + o_b).astype(BF).astype(F32)
        st_a[pl.ds(g, STRIDE)] = s_a
        st_b[pl.ds(g, STRIDE)] = s_b
        put(g, *normed(s_a, s_b, gain_a, gain_b))

    def second_state(m, g, o_a, o_b):
        s_a, s_b = st_a[pl.ds(g, STRIDE)], st_b[pl.ds(g, STRIDE)]
        t_a = (s_a + o_a).astype(BF)
        t_b = (s_b + o_b).astype(BF)

        @pl.when(m < 16)
        def _():
            r = pl.multiple_of(32 * m, 32)
            fin[0, pl.ds(r, 32), 0:128] = t_a[16:48]
            fin[0, pl.ds(r, 32), 128:256] = t_b[16:48]

        y_a, y_b = oc_a[pl.ds(g, STRIDE)], oc_b[pl.ds(g, STRIDE)]
        mask = y_b[:, 32:33]
        put(
            g,
            (y_a + 0.5 * (s_a + t_a.astype(F32))) * mask,
            (y_b + 0.5 * (s_b + t_b.astype(F32))) * mask,
        )

    def mixed(m, g, o_a, o_b):
        n_a, n_b = normed(
            o_a.astype(BF).astype(F32), o_b.astype(BF).astype(F32), ocean_a, ocean_b
        )

        @pl.when(m < 16)
        def _():
            r = pl.multiple_of(32 * m, 32)
            nrm[pl.ds(r, 32), 0:128] = n_a[16:48].astype(BF)
            nrm[pl.ds(r, 32), 128:256] = n_b[16:48].astype(BF)

    convolve(20, 0, hidden)
    replicate()
    loads[4].wait()
    pair[3].wait_recv()
    prepare(1)
    convolve(19, 1, first_state)
    replicate()
    convolve(18, 0, hidden)
    replicate()
    convolve(17, 1, second_state)
    replicate()
    loads[5].wait()
    pair[4].wait_recv()
    prepare(2)
    convolve(16, 2, mixed)

    loads[6].wait()
    loads[7].wait()

    @pl.loop(0, 2)
    def _(m):
        r = pl.multiple_of(256 * m, 256)
        h = jnp.dot(nrm[pl.ds(r, 256), :][:, :160], miv[...], preferred_element_type=F32)
        h = gelu(h).astype(BF)
        u = lax.dot_general(h, mov[...], NT, preferred_element_type=F32).astype(BF)
        fin[1, pl.ds(r, 256), 0:160] = u

    for b in range(2):
        q = pl.multiple_of(256 * jnp.where(c == 0, b, 3 - b), 256)
        o = pl.multiple_of(256 * jnp.where(c == 0, b, 1 - b), 256)
        t_a = lax.dot_general(
            fin[0, 256 * b : 256 * b + 256][:, :160], tsel[b], TN, preferred_element_type=F32
        )
        u = lax.dot_general(
            fin[1, 256 * b : 256 * b + 256][:, :160], tsel[b], TN, preferred_element_type=F32
        )
        w_row = wet[:, pl.ds(q, 256)].astype(F32)
        for k in range(2):
            rows = slice(80 * k, 80 * k + 80)
            obuf[0, k, :, pl.ds(o, 256)] = t_a[rows].astype(BF)
            obuf[1, k, :, pl.ds(o, 256)] = (
                xo[k, :, pl.ds(q, 256)].astype(F32) + w_row * u[rows]
            ).astype(BF)

    mine = pl.ds(pl.multiple_of(512 * c, 512), 512)
    outs = []
    for n, ref in enumerate((out_a, out_o)):
        outs.append(
            pltpu.make_async_remote_copy(
                src_ref=obuf.at[n, pc],
                dst_ref=ref.at[:, mine],
                send_sem=osem_s.at[n],
                recv_sem=osem_r.at[n],
                device_id=partner,
                device_id_type=MESH,
            )
        )
    for copy in outs:
        copy.start()
    out_a[:, mine] = obuf[0, c]
    out_o[:, mine] = obuf[1, c]
    for copy in halo_copies:
        copy.wait_send()
    for copy in pair:
        copy.wait_send()
    for copy in outs:
        copy.wait()


def per_device(
    atm_state, ocean_state, wet_mask, neighbours, west_rim, east_rim, atm_gain,
    atm_conv_in, atm_conv_out, ocean_conv, ocean_gain, mlp_in, mlp_out,
):
    vmem = pl.BlockSpec(memory_space=pltpu.VMEM)
    anym = pl.BlockSpec(memory_space=pl.ANY)
    pixels = atm_state.shape[1]
    taps = [jnp.transpose(w, (1, 0, 2)) for w in (atm_conv_in, atm_conv_out, ocean_conv)]
    out = jax.ShapeDtypeStruct((CH, pixels), BF)
    dma = pltpu.SemaphoreType.DMA
    return pl.pallas_call(
        kernel,
        name="coupled_step",
        out_shape=(out, out),
        in_specs=[anym] + [vmem] * 3 + [anym] * 7,
        out_specs=(vmem, vmem),
        scratch_shapes=[
            pltpu.VMEM((2, CH, pixels), BF),
            pltpu.VMEM((2, CH, pixels), BF),
            pltpu.VMEM((3, 2, 9, CH, C), BF),
            pltpu.VMEM((3, 512, 512), BF),
            pltpu.VMEM((C, 640), BF),
            pltpu.VMEM((C, 640), BF),
            pltpu.VMEM((2, 8, pixels), jnp.int32),
            pltpu.VMEM((3, 256, 256), BF),
            pltpu.VMEM((2, 2, 96, 128), BF),
            pltpu.VMEM((2, 96, 256), BF),
            pltpu.VMEM((BUF, 128), F32),
            pltpu.VMEM((BUF, 128), F32),
            pltpu.VMEM((BUF, 128), F32),
            pltpu.VMEM((BUF, 128), F32),
            pltpu.VMEM((BUF, 128), BF),
            pltpu.VMEM((BUF, 128), F32),
            pltpu.VMEM((BUF, 128), BF),
            pltpu.VMEM((BUF, 512), F32),
            pltpu.VMEM((512, 256), BF),
            pltpu.VMEM((2, 512, 256), BF),
            pltpu.VMEM((2, 2, CH, 512), BF),
            pltpu.VMEM((8, pixels), jnp.int32),
            dma((8,)),
            dma((5,)),
            dma((5,)),
            dma((4,)),
            dma((2, 2)),
            dma((2,)),
            dma((2,)),
        ],
        compiler_params=pltpu.CompilerParams(
            collective_id=0, has_side_effects=True, vmem_limit_bytes=48 * 1024 * 1024
        ),
    )(
        neighbours,
        wet_mask.reshape(1, pixels),
        atm_gain.reshape(1, C),
        ocean_gain.reshape(1, C),
        atm_state,
        ocean_state,
        *taps,
        jnp.transpose(mlp_in),
        mlp_out,
    )


def solution(mesh):
    in_specs = (
        P("chan", "sector"),
        P("chan", "sector"),
        P("sector"),
        P(None, "sector"),
        P("sector"),
        P("sector"),
        P(),
        P("chan", None, None),
        P("chan", None, None),
        P("chan", None, None),
        P(),
        P(),
        P(),
    )
    out_specs = (P("chan", "sector"), P("chan", "sector"))
    return jax.shard_map(
        per_device, mesh=mesh, in_specs=in_specs, out_specs=out_specs, check_vma=False
    )
```

```python
import functools

import jax
import jax.numpy as jnp
from jax import lax
from jax.experimental import pallas as pl
from jax.experimental.pallas import tpu as pltpu
from jax.sharding import PartitionSpec as P

EPSILON = 1e-06
CH = 80
C = 160
ROWS = 32
STRIDE = 48
BUF = 1104
BC = BUF + 96
MESH = pl.DeviceIdType.MESH
NT = (((1,), (1,)), ((), ()))
TN = (((0,), (0,)), ((), ()))
F32 = jnp.float32
BF = jnp.bfloat16


def iota(shape, dim):
    return lax.broadcasted_iota(jnp.int32, shape, dim)


def onehot(hit):
    return jnp.where(hit, 1.0, 0.0).astype(BF)


def tap_slot(dyi, dxi):
    m = 3 * dyi + dxi
    return 0 if m == 4 else (m + 1 if m < 4 else m)


def kernel(
    nb, wet, ga, go, atm, oc, w1, w2, w3, mi, mo,
    out_a, out_o,
    xa, xo, wraw, wb, miv, mov, keys, tsel, sbuf, halo, st_a, st_b, oc_a, oc_b,
    va, bc, pbuf, nrm, fin, obuf, nbv,
    lsem, psem_s, psem_r, hsem_s, hsem_r, osem_s, osem_r,
):
    sectors = lax.axis_size("sector")
    s = lax.axis_index("sector")
    c = lax.axis_index("chan")
    pc = 1 - c
    west = lax.rem(s + sectors - 1, sectors)
    east = lax.rem(s + 1, sectors)
    partner = {"sector": s, "chan": pc}

    bar = pltpu.get_barrier_semaphore()
    pl.semaphore_signal(bar, inc=1, device_id=partner, device_id_type=MESH)
    for chip in (west, east):
        for t in range(2):
            pl.semaphore_signal(
                bar, inc=1, device_id={"sector": chip, "chan": t}, device_id_type=MESH
            )

    loads = [
        pltpu.make_async_copy(nb, nbv, lsem.at[0]),
        pltpu.make_async_copy(atm, xa.at[c], lsem.at[1]),
        pltpu.make_async_copy(oc, xo.at[c], lsem.at[2]),
        pltpu.make_async_copy(w1, wraw.at[0, c], lsem.at[3]),
        pltpu.make_async_copy(w2, wraw.at[1, c], lsem.at[4]),
        pltpu.make_async_copy(w3, wraw.at[2, c], lsem.at[5]),
        pltpu.make_async_copy(mi, miv, lsem.at[6]),
        pltpu.make_async_copy(mo, mov, lsem.at[7]),
    ]
    for load in loads:
        load.start()
    loads[0].wait()

    for b in range(8):
        lane = iota((8, 128), 1)
        v = jnp.broadcast_to(nbv[3:4, 128 * b : 128 * b + 128], (8, 128))
        inside = v < 1024
        hop = jnp.where(inside, v - 128 * b, lane)
        col = jnp.where(inside, 1, 0)
        for _ in range(5):
            col = col + jnp.take_along_axis(col, hop, axis=1, mode="promise_in_bounds")
            hop = jnp.take_along_axis(hop, hop, axis=1, mode="promise_in_bounds")
        cyc = 4 * b + lax.shift_right_logical(lane, 5)
        keys[0, :, 128 * b : 128 * b + 128] = 32 * cyc + col
        keys[1, :, 128 * b : 128 * b + 128] = 32 * (31 - cyc) + col

    loads[1].wait()
    loads[2].wait()

    wet16 = jnp.broadcast_to(wet[...], (16, 1024)).astype(F32).astype(BF)

    hr = iota((256, 256), 0)
    hh = hr & 127
    far = hr >= 128
    hi = lax.shift_right_logical(hh * 205, 10)
    he = hh - 5 * hi
    key_a = jnp.where(hh < 105, 32 * hi + jnp.where(far, 27 + he, he), -1)
    key_o = jnp.where(
        (hh >= 105) & (hh < 122), 32 * (hh - 105) + jnp.where(far, 31, 0), -1
    )
    z16 = jnp.zeros((16, 256), BF)
    for t in range(2):
        total = jnp.zeros((96, 256), F32)
        for b in range(3):
            q = 256 * (b if t == 0 else 3 - b)
            key_q = keys[t, 0:1, q : q + 256]
            x_a = jnp.concatenate([xa[c, :, q : q + 256], z16], axis=0)
            x_o = jnp.concatenate([xo[c, :, q : q + 256], wet16[:, q : q + 256]], axis=0)
            total = total + lax.dot_general(
                x_a, onehot(key_a == key_q), NT, preferred_element_type=F32
            )
            total = total + lax.dot_general(
                x_o, onehot(key_o == key_q), NT, preferred_element_type=F32
            )
        sbuf[t, 0] = total[:, :128].astype(BF)
        sbuf[t, 1] = total[:, 128:].astype(BF)

    pl.semaphore_wait(bar, 5)

    halo_copies = []
    for t in range(2):
        for d, chip in ((0, west), (1, east)):
            halo_copies.append(
                pltpu.make_async_remote_copy(
                    src_ref=sbuf.at[t, d],
                    dst_ref=halo.at[c, :, pl.ds(128 * d, 128)],
                    send_sem=hsem_s.at[2 * t + d],
                    recv_sem=hsem_r.at[d, c],
                    device_id={"sector": chip, "chan": t},
                    device_id_type=MESH,
                )
            )
    for copy in halo_copies:
        copy.start()

    def to_partner(src, dst, n):
        return pltpu.make_async_remote_copy(
            src_ref=src,
            dst_ref=dst,
            send_sem=psem_s.at[n],
            recv_sem=psem_r.at[n],
            device_id=partner,
            device_id_type=MESH,
        )

    window = pl.ds(pl.multiple_of(256 * pc, 256), 768)
    pair = [
        to_partner(atm.at[:, window], xa.at[c, :, window], 0),
        to_partner(w1, wraw.at[0, c], 1),
        to_partner(oc.at[:, window], xo.at[c, :, window], 2),
        to_partner(w2, wraw.at[1, c], 3),
        to_partner(w3, wraw.at[2, c], 4),
    ]
    for copy in pair:
        copy.start()

    for b in range(3):
        q = pl.multiple_of(256 * jnp.where(c == 0, b, 3 - b), 256)
        key_q = keys[c, 0:1, pl.ds(q, 256)] - 256 * b
        tsel[b] = onehot(iota((256, 256), 0) == key_q)

    def prepare(n):
        wb[n, :, 480:512] = jnp.zeros((512, 32), BF)
        wb[n, 480:512, :] = jnp.zeros((32, 512), BF)
        for dyi in range(3):
            for dxi in range(3):
                k = jnp.where(c == 0, tap_slot(dyi, dxi), tap_slot(2 - dyi, dxi))
                w_0 = wraw[n, 0, k]
                w_1 = wraw[n, 1, k]
                for lanes, dst, width in (
                    (slice(0, 128), 128 * dyi, 128),
                    (slice(128, 160), 384 + 32 * dyi, 32),
                ):
                    r = 128 * dxi
                    wb[n, r : r + 80, dst : dst + width] = w_0[:, lanes]
                    wb[n, r + 80 : r + 128, dst : dst + width] = w_1[0:48, lanes]
                    r = 384 + 32 * dxi
                    wb[n, r : r + 32, dst : dst + width] = w_1[48:80, lanes]

    loads[3].wait()
    pair[1].wait_recv()
    prepare(0)

    gain_a = ga[:, 0:128]
    gain_b = jnp.concatenate([ga[:, 128:160]] * 4, axis=1)
    ocean_a = go[:, 0:128]
    ocean_b = jnp.concatenate([go[:, 128:160]] * 4, axis=1)

    pair[0].wait_recv()
    pair[2].wait_recv()
    for b in range(3):
        q = pl.multiple_of(256 * jnp.where(c == 0, b, 3 - b), 256)
        x_1 = xa[1, :, pl.ds(q, 256)]
        x_a = jnp.concatenate(
            [xa[0, :, pl.ds(q, 256)], x_1] + [x_1[48:80]] * 3, axis=0
        )
        wet_b = jnp.broadcast_to(wet[:, pl.ds(q, 256)], (32, 256)).astype(F32).astype(BF)
        x_1 = xo[1, :, pl.ds(q, 256)]
        x_o = jnp.concatenate(
            [xo[0, :, pl.ds(q, 256)], x_1] + [x_1[48:80]] * 2 + [wet_b], axis=0
        )
        v_a = lax.dot_general(tsel[b], x_a, NT, preferred_element_type=F32)
        v_o = lax.dot_general(tsel[b], x_o, NT, preferred_element_type=F32)
        for il in range(8):
            i = 8 * b + il
            rows = slice(32 * il, 32 * il + 32)
            for g in [STRIDE * (i + 1) + 16] + ([16] if i == 0 else []):
                if i <= 20:
                    st_a[g : g + 32] = v_a[rows, :128]
                    st_b[g : g + 32] = v_a[rows, 128:]
                if i <= 16:
                    oc_a[g : g + 32] = v_o[rows, :128]
                    oc_b[g : g + 32] = v_o[rows, 128:]

    for d in range(2):
        for sender in range(2):
            pltpu.make_async_remote_copy(
                src_ref=sbuf.at[0, d],
                dst_ref=halo.at[sender, :, pl.ds(128 * d, 128)],
                send_sem=hsem_s.at[0],
                recv_sem=hsem_r.at[d, sender],
                device_id=partner,
                device_id_type=MESH,
            ).wait_recv()
    h_1 = halo[1, 48:80]
    h_atm = jnp.concatenate([halo[0, 0:80], halo[1, 0:80]] + [h_1] * 3, axis=0)
    h_oc = jnp.concatenate(
        [halo[0, 0:80], halo[1, 0:80]] + [h_1] * 2 + [halo[0, 80:96]] * 2, axis=0
    )
    hl = iota((1, 256), 1)
    hh = hl & 127
    far = hl >= 128
    hi = lax.shift_right_logical(hh * 205, 10)
    he = hh - 5 * hi
    p1 = jnp.where(hh < 105, jnp.where(far, 16 * hi + 27 + he, 16 * hi + 32 + he), -1)
    p2 = jnp.where(hi == 0, p1 - 16, p1)
    r = iota((368, 256), 0)
    v_a = lax.dot_general(
        onehot((r == p1) | (r == p2)), h_atm, NT, preferred_element_type=F32
    )
    oi = hh - 105
    p1 = jnp.where(
        (oi >= 0) & (oi < 17), jnp.where(far, 16 * oi + 31, 16 * oi + 32), -1
    )
    p2 = jnp.where(oi == 0, p1 - 16, p1)
    r = iota((304, 256), 0)
    v_o = lax.dot_general(
        onehot((r == p1) | (r == p2)), h_oc, NT, preferred_element_type=F32
    )
    for k in range(23):
        rows = slice(16 * k, 16 * k + 16)
        g = STRIDE * k
        st_a[g : g + 16] = v_a[rows, :128]
        st_b[g : g + 16] = v_a[rows, 128:]
        if k < 19:
            oc_a[g : g + 16] = v_o[rows, :128]
            oc_b[g : g + 16] = v_o[rows, 128:]

    group = lax.shift_right_logical(iota((1, 128), 1), 5)

    def normed(x_a, x_b, scale_a, scale_b):
        mean_sq = jnp.sum(x_a * x_a + 0.25 * (x_b * x_b), axis=1, keepdims=True) * (1.0 / C)
        inv = lax.rsqrt(mean_sq + EPSILON)
        return x_a * inv * scale_a, x_b * inv * scale_b

    def put(g, x_a, x_b, rows=STRIDE):
        va[pl.ds(g, rows)] = x_a.astype(BF)
        y = x_b.astype(BF)
        bc[pl.ds(g + 2 * STRIDE, rows), 0:32] = y[:, 0:32]
        bc[pl.ds(g + STRIDE, rows), 32:64] = y[:, 32:64]
        bc[pl.ds(g, rows), 64:96] = y[:, 64:96]

    bc[:, 96:128] = jnp.zeros((BC, 32), BF)

    @pl.loop(0, 22, unroll=True)
    def _(m):
        g = pl.multiple_of(STRIDE * m, STRIDE)
        put(g, *normed(st_a[pl.ds(g, STRIDE)], st_b[pl.ds(g, STRIDE)], gain_a, gain_b))

    put(1056, *normed(st_a[1056:1072], st_b[1056:1072], gain_a, gain_b), rows=16)

    def convolve(n, wi, epilogue):
        size = 16 + STRIDE * n
        lhs = jnp.concatenate(
            [va[0:size], va[48 : 48 + size], va[96 : 96 + size], bc[96 : 96 + size]], axis=1
        )
        pbuf[48 : 48 + size] = lax.dot_general(lhs, wb[wi], NT, preferred_element_type=F32)

        @pl.loop(0, n + 1, unroll=True)
        def _(m):
            g = pl.multiple_of(STRIDE * m + STRIDE, STRIDE)
            x = pbuf[pl.ds(g - 8, STRIDE + 16)]
            mid = slice(8, 8 + STRIDE)
            p_b = x[:, 384:512]
            out_a = (
                x[mid, 128:256]
                + pltpu.roll(x[:, 0:128], 1, 0)[mid]
                + pltpu.roll(x[:, 256:384], STRIDE + 15, 0)[mid]
            )
            y = jnp.where(group == 0, pltpu.roll(p_b, 1, 0)[mid], 0.0)
            y = jnp.where(group == 1, p_b[mid], y)
            y = jnp.where(group == 2, pltpu.roll(p_b, STRIDE + 15, 0)[mid], y)
            y = y + pltpu.roll(y, 64, 1)
            epilogue(m, g, out_a, y + pltpu.roll(y, 32, 1))

    def replicate():
        first = iota((16, 128), 0) < 8

        def mix(own, nxt):
            mask = first[:, : own.shape[1]]
            return jnp.where(mask, nxt.astype(F32), own.astype(F32)).astype(BF)

        for ref, at, lanes in (
            (va, 0, slice(0, 128)),
            (bc, 96, slice(0, 32)),
            (bc, 48, slice(32, 64)),
            (bc, 0, slice(64, 96)),
        ):
            own, nxt = ref[at + 48 : at + 64, lanes], ref[at + 96 : at + 112, lanes]
            ref[at : at + 16, lanes] = own
            ref[at + 16 : at + 48, lanes] = ref[at + 64 : at + 96, lanes]
            ref[at + 48 : at + 64, lanes] = mix(own, nxt)

    def gelu(x):
        return jax.nn.gelu(x, approximate=True)

    def hidden(m, g, o_a, o_b):
        put(g, gelu(o_a), gelu(o_b))

    def first_state(m, g, o_a, o_b):
        s_a = (st_a[pl.ds(g, STRIDE)] + o_a).astype(BF).astype(F32)
        s_b = (st_b[pl.ds(g, STRIDE)] + o_b).astype(BF).astype(F32)
        st_a[pl.ds(g, STRIDE)] = s_a
        st_b[pl.ds(g, STRIDE)] = s_b
        put(g, *normed(s_a, s_b, gain_a, gain_b))

    def second_state(m, g, o_a, o_b):
        s_a, s_b = st_a[pl.ds(g, STRIDE)], st_b[pl.ds(g, STRIDE)]
        t_a = (s_a + o_a).astype(BF)
        t_b = (s_b + o_b).astype(BF)
        r = pl.multiple_of(32 * m, 32)
        fin[0, pl.ds(r, 32), 0:128] = t_a[16:48]
        fin[0, pl.ds(r, 32), 128:256] = t_b[16:48]
        y_a, y_b = oc_a[pl.ds(g, STRIDE)], oc_b[pl.ds(g, STRIDE)]
        mask = y_b[:, 96:97]
        put(
            g,
            (y_a + 0.5 * (s_a + t_a.astype(F32))) * mask,
            (y_b + 0.5 * (s_b + t_b.astype(F32))) * mask,
        )

    def mixed(m, g, o_a, o_b):
        n_a, n_b = normed(
            o_a.astype(BF).astype(F32), o_b.astype(BF).astype(F32), ocean_a, ocean_b
        )
        r = pl.multiple_of(32 * m, 32)
        nrm[pl.ds(r, 32), 0:128] = n_a[16:48].astype(BF)
        nrm[pl.ds(r, 32), 128:256] = n_b[16:48].astype(BF)

    convolve(20, 0, hidden)
    replicate()
    loads[4].wait()
    pair[3].wait_recv()
    prepare(1)
    convolve(19, 1, first_state)
    replicate()
    convolve(18, 0, hidden)
    replicate()
    convolve(17, 1, second_state)
    replicate()
    loads[5].wait()
    pair[4].wait_recv()
    prepare(2)
    convolve(16, 2, mixed)

    loads[6].wait()
    loads[7].wait()

    @pl.loop(0, 2)
    def _(m):
        r = pl.multiple_of(256 * m, 256)
        h = jnp.dot(nrm[pl.ds(r, 256), :][:, :160], miv[...], preferred_element_type=F32)
        h = gelu(h).astype(BF)
        u = lax.dot_general(h, mov[...], NT, preferred_element_type=F32).astype(BF)
        fin[1, pl.ds(r, 256), 0:160] = u

    for b in range(2):
        q = pl.multiple_of(256 * jnp.where(c == 0, b, 3 - b), 256)
        o = pl.multiple_of(256 * jnp.where(c == 0, b, 1 - b), 256)
        t_a = lax.dot_general(
            fin[0, 256 * b : 256 * b + 256][:, :160], tsel[b], TN, preferred_element_type=F32
        )
        u = lax.dot_general(
            fin[1, 256 * b : 256 * b + 256][:, :160], tsel[b], TN, preferred_element_type=F32
        )
        w_row = wet[:, pl.ds(q, 256)].astype(F32)
        for k in range(2):
            rows = slice(80 * k, 80 * k + 80)
            obuf[0, k, :, pl.ds(o, 256)] = t_a[rows].astype(BF)
            obuf[1, k, :, pl.ds(o, 256)] = (
                xo[k, :, pl.ds(q, 256)].astype(F32) + w_row * u[rows]
            ).astype(BF)

    mine = pl.ds(pl.multiple_of(512 * c, 512), 512)
    outs = []
    for n, ref in enumerate((out_a, out_o)):
        outs.append(
            pltpu.make_async_remote_copy(
                src_ref=obuf.at[n, pc],
                dst_ref=ref.at[:, mine],
                send_sem=osem_s.at[n],
                recv_sem=osem_r.at[n],
                device_id=partner,
                device_id_type=MESH,
            )
        )
    for copy in outs:
        copy.start()
    out_a[:, mine] = obuf[0, c]
    out_o[:, mine] = obuf[1, c]
    for copy in halo_copies:
        copy.wait_send()
    for copy in pair:
        copy.wait_send()
    for copy in outs:
        copy.wait()


def per_device(
    atm_state, ocean_state, wet_mask, neighbours, west_rim, east_rim, atm_gain,
    atm_conv_in, atm_conv_out, ocean_conv, ocean_gain, mlp_in, mlp_out,
):
    vmem = pl.BlockSpec(memory_space=pltpu.VMEM)
    anym = pl.BlockSpec(memory_space=pl.ANY)
    pixels = atm_state.shape[1]
    taps = [jnp.transpose(w, (1, 0, 2)) for w in (atm_conv_in, atm_conv_out, ocean_conv)]
    out = jax.ShapeDtypeStruct((CH, pixels), BF)
    dma = pltpu.SemaphoreType.DMA
    return pl.pallas_call(
        kernel,
        name="coupled_step",
        out_shape=(out, out),
        in_specs=[anym] + [vmem] * 3 + [anym] * 7,
        out_specs=(vmem, vmem),
        scratch_shapes=[
            pltpu.VMEM((2, CH, pixels), BF),
            pltpu.VMEM((2, CH, pixels), BF),
            pltpu.VMEM((3, 2, 9, CH, C), BF),
            pltpu.VMEM((3, 512, 512), BF),
            pltpu.VMEM((C, 640), BF),
            pltpu.VMEM((C, 640), BF),
            pltpu.VMEM((2, 8, pixels), jnp.int32),
            pltpu.VMEM((3, 256, 256), BF),
            pltpu.VMEM((2, 2, 96, 128), BF),
            pltpu.VMEM((2, 96, 256), BF),
            pltpu.VMEM((BUF, 128), F32),
            pltpu.VMEM((BUF, 128), F32),
            pltpu.VMEM((BUF, 128), F32),
            pltpu.VMEM((BUF, 128), F32),
            pltpu.VMEM((BUF, 128), BF),
            pltpu.VMEM((BC, 128), BF),
            pltpu.VMEM((BUF, 512), F32),
            pltpu.VMEM((576, 256), BF),
            pltpu.VMEM((2, 576, 256), BF),
            pltpu.VMEM((2, 2, CH, 512), BF),
            pltpu.VMEM((8, pixels), jnp.int32),
            dma((8,)),
            dma((5,)),
            dma((5,)),
            dma((4,)),
            dma((2, 2)),
            dma((2,)),
            dma((2,)),
        ],
        compiler_params=pltpu.CompilerParams(
            collective_id=0, has_side_effects=True, vmem_limit_bytes=67_043_328
        ),
    )(
        neighbours,
        wet_mask.reshape(1, pixels),
        atm_gain.reshape(1, C),
        ocean_gain.reshape(1, C),
        atm_state,
        ocean_state,
        *taps,
        jnp.transpose(mlp_in),
        mlp_out,
    )


def solution(mesh):
    in_specs = (
        P("chan", "sector"),
        P("chan", "sector"),
        P("sector"),
        P(None, "sector"),
        P("sector"),
        P("sector"),
        P(),
        P("chan", None, None),
        P("chan", None, None),
        P("chan", None, None),
        P(),
        P(),
        P(),
    )
    out_specs = (P("chan", "sector"), P("chan", "sector"))
    return jax.shard_map(
        per_device, mesh=mesh, in_specs=in_specs, out_specs=out_specs, check_vma=False
    )
```

```python
import functools

import jax
import jax.numpy as jnp
from jax import lax
from jax.experimental import pallas as pl
from jax.experimental.pallas import tpu as pltpu
from jax.sharding import PartitionSpec as P

EPSILON = 1e-06
CH = 80
C = 160
ROWS = 32
STRIDE = 48
BUF = 1104
BC = BUF + 96
GROUP = 10
AHEAD = 2
MESH = pl.DeviceIdType.MESH
NT = (((1,), (1,)), ((), ()))
TN = (((0,), (0,)), ((), ()))
F32 = jnp.float32
BF = jnp.bfloat16


def iota(shape, dim):
    return lax.broadcasted_iota(jnp.int32, shape, dim)


def onehot(hit):
    return jnp.where(hit, 1.0, 0.0).astype(BF)


def tap_slot(dyi, dxi):
    m = 3 * dyi + dxi
    return 0 if m == 4 else (m + 1 if m < 4 else m)


def kernel(
    nb, wet_h, ga_h, go_h, atm, oc, w1, w2, w3, mi, mo,
    out_a, out_o,
    xa, xo, wraw, wb, miv, mov, keys, tsel, sbuf, halo, st_a, st_b, oc_a, oc_b,
    va, bc, pbuf, nrm, fin, obuf, nbv, wet, ga, go, hsel, osel,
    lsem, psem_s, psem_r, hsem_s, hsem_r, osem_s, osem_r,
):
    sectors = lax.axis_size("sector")
    s = lax.axis_index("sector")
    c = lax.axis_index("chan")
    pc = 1 - c
    west = lax.rem(s + sectors - 1, sectors)
    east = lax.rem(s + 1, sectors)
    partner = {"sector": s, "chan": pc}

    bar = pltpu.get_barrier_semaphore()
    pl.semaphore_signal(bar, inc=1, device_id=partner, device_id_type=MESH)
    for chip in (west, east):
        for t in range(2):
            pl.semaphore_signal(
                bar, inc=1, device_id={"sector": chip, "chan": t}, device_id_type=MESH
            )

    loads = [
        pltpu.make_async_copy(nb, nbv, lsem.at[0]),
        pltpu.make_async_copy(atm, xa.at[c], lsem.at[1]),
        pltpu.make_async_copy(oc, xo.at[c], lsem.at[2]),
        pltpu.make_async_copy(w1, wraw.at[0, c], lsem.at[3]),
        pltpu.make_async_copy(w2, wraw.at[1, c], lsem.at[4]),
        pltpu.make_async_copy(w3, wraw.at[2, c], lsem.at[5]),
        pltpu.make_async_copy(mi, miv, lsem.at[6]),
        pltpu.make_async_copy(mo, mov, lsem.at[7]),
        pltpu.make_async_copy(wet_h, wet, lsem.at[8]),
        pltpu.make_async_copy(ga_h, ga, lsem.at[9]),
        pltpu.make_async_copy(go_h, go, lsem.at[10]),
    ]
    for load in loads:
        load.start()
    loads[0].wait()

    for b in range(8):
        lane = iota((8, 128), 1)
        v = jnp.broadcast_to(nbv[3:4, 128 * b : 128 * b + 128], (8, 128))
        inside = v < 1024
        hop = jnp.where(inside, v - 128 * b, lane)
        col = jnp.where(inside, 1, 0)
        for _ in range(5):
            col = col + jnp.take_along_axis(col, hop, axis=1, mode="promise_in_bounds")
            hop = jnp.take_along_axis(hop, hop, axis=1, mode="promise_in_bounds")
        cyc = 4 * b + lax.shift_right_logical(lane, 5)
        keys[0, :, 128 * b : 128 * b + 128] = 32 * cyc + col
        keys[1, :, 128 * b : 128 * b + 128] = 32 * (31 - cyc) + col

    loads[1].wait()
    loads[2].wait()
    loads[8].wait()

    wet16 = jnp.broadcast_to(wet[...], (16, 1024)).astype(F32).astype(BF)

    hr = iota((256, 256), 0)
    hh = hr & 127
    far = hr >= 128
    hi = lax.shift_right_logical(hh * 205, 10)
    he = hh - 5 * hi
    key_a = jnp.where(hh < 105, 32 * hi + jnp.where(far, 27 + he, he), -1)
    key_o = jnp.where(
        (hh >= 105) & (hh < 122), 32 * (hh - 105) + jnp.where(far, 31, 0), -1
    )
    z16 = jnp.zeros((16, 256), BF)
    for t in range(2):
        total = jnp.zeros((96, 256), F32)
        for b in range(3):
            q = 256 * (b if t == 0 else 3 - b)
            key_q = keys[t, 0:1, q : q + 256]
            x_a = jnp.concatenate([xa[c, :, q : q + 256], z16], axis=0)
            x_o = jnp.concatenate([xo[c, :, q : q + 256], wet16[:, q : q + 256]], axis=0)
            total = total + lax.dot_general(
                x_a, onehot(key_a == key_q), NT, preferred_element_type=F32
            )
            total = total + lax.dot_general(
                x_o, onehot(key_o == key_q), NT, preferred_element_type=F32
            )
        sbuf[t, 0] = total[:, :128].astype(BF)
        sbuf[t, 1] = total[:, 128:].astype(BF)

    pl.semaphore_wait(bar, 5)

    halo_copies = []
    for t in range(2):
        for d, chip in ((0, west), (1, east)):
            halo_copies.append(
                pltpu.make_async_remote_copy(
                    src_ref=sbuf.at[t, d],
                    dst_ref=halo.at[c, :, pl.ds(128 * d, 128)],
                    send_sem=hsem_s.at[2 * t + d],
                    recv_sem=hsem_r.at[d, c],
                    device_id={"sector": chip, "chan": t},
                    device_id_type=MESH,
                )
            )
    for copy in halo_copies:
        copy.start()

    def to_partner(src, dst, n):
        return pltpu.make_async_remote_copy(
            src_ref=src,
            dst_ref=dst,
            send_sem=psem_s.at[n],
            recv_sem=psem_r.at[n],
            device_id=partner,
            device_id_type=MESH,
        )

    window = pl.ds(pl.multiple_of(256 * pc, 256), 768)
    pair = [
        to_partner(atm.at[:, window], xa.at[c, :, window], 0),
        to_partner(w1, wraw.at[0, c], 1),
        to_partner(oc.at[:, window], xo.at[c, :, window], 2),
        to_partner(w2, wraw.at[1, c], 3),
        to_partner(w3, wraw.at[2, c], 4),
    ]
    for copy in pair:
        copy.start()

    for b in range(3):
        q = pl.multiple_of(256 * jnp.where(c == 0, b, 3 - b), 256)
        key_q = keys[c, 0:1, pl.ds(q, 256)] - 256 * b
        tsel[b] = onehot(iota((256, 256), 0) == key_q)

    def prepare(n):
        wb[n, :, 480:512] = jnp.zeros((512, 32), BF)
        wb[n, 480:512, :] = jnp.zeros((32, 512), BF)
        for dyi in range(3):
            for dxi in range(3):
                k = jnp.where(c == 0, tap_slot(dyi, dxi), tap_slot(2 - dyi, dxi))
                w_0 = wraw[n, 0, k]
                w_1 = wraw[n, 1, k]
                for lanes, dst, width in (
                    (slice(0, 128), 128 * dyi, 128),
                    (slice(128, 160), 384 + 32 * dyi, 32),
                ):
                    r = 128 * dxi
                    wb[n, r : r + 80, dst : dst + width] = w_0[:, lanes]
                    wb[n, r + 80 : r + 128, dst : dst + width] = w_1[0:48, lanes]
                    r = 384 + 32 * dxi
                    wb[n, r : r + 32, dst : dst + width] = w_1[48:80, lanes]

    hl = iota((1, 256), 1)
    hh = hl & 127
    far = hl >= 128
    hi = lax.shift_right_logical(hh * 205, 10)
    he = hh - 5 * hi
    p1 = jnp.where(hh < 105, jnp.where(far, 16 * hi + 27 + he, 16 * hi + 32 + he), -1)
    p2 = jnp.where(hi == 0, p1 - 16, p1)
    r = iota((368, 256), 0)
    hsel[...] = onehot((r == p1) | (r == p2))
    oi = hh - 105
    p1 = jnp.where((oi >= 0) & (oi < 17), jnp.where(far, 16 * oi + 31, 16 * oi + 32), -1)
    p2 = jnp.where(oi == 0, p1 - 16, p1)
    r = iota((304, 256), 0)
    osel[...] = onehot((r == p1) | (r == p2))

    loads[9].wait()
    loads[10].wait()
    gain_a = ga[:, 0:128]
    gain_b = jnp.concatenate([ga[:, 128:160]] * 4, axis=1)
    ocean_a = go[:, 0:128]
    ocean_b = jnp.concatenate([go[:, 128:160]] * 4, axis=1)

    def normed(x_a, x_b, scale_a, scale_b):
        mean_sq = jnp.sum(x_a * x_a + 0.25 * (x_b * x_b), axis=1, keepdims=True) * (1.0 / C)
        inv = lax.rsqrt(mean_sq + EPSILON)
        return x_a * inv * scale_a, x_b * inv * scale_b

    def put(v, g, x_a, x_b, rows=STRIDE):
        va[v, pl.ds(g, rows)] = x_a.astype(BF)
        y = x_b.astype(BF)
        bc[v, pl.ds(g + 2 * STRIDE, rows), 0:32] = y[:, 0:32]
        bc[v, pl.ds(g + STRIDE, rows), 32:64] = y[:, 32:64]
        bc[v, pl.ds(g, rows), 64:96] = y[:, 64:96]

    for v in range(2):
        bc[v, :, 96:128] = jnp.zeros((BC, 32), BF)

    pair[0].wait_recv()
    for b in range(3):
        q = pl.multiple_of(256 * jnp.where(c == 0, b, 3 - b), 256)
        x_1 = xa[1, :, pl.ds(q, 256)]
        x_a = jnp.concatenate([xa[0, :, pl.ds(q, 256)], x_1] + [x_1[48:80]] * 3, axis=0)
        v_a = lax.dot_general(tsel[b], x_a, NT, preferred_element_type=F32)
        for il in range(8):
            i = 8 * b + il
            rows = slice(32 * il, 32 * il + 32)
            if i <= 20:
                n_a, n_b = normed(v_a[rows, :128], v_a[rows, 128:], gain_a, gain_b)
            for g in [STRIDE * (i + 1) + 16] + ([16] if i == 0 else []):
                if i <= 20:
                    st_a[g : g + 32] = v_a[rows, :128]
                    st_b[g : g + 32] = v_a[rows, 128:]
                    put(0, g, n_a, n_b, rows=32)

    loads[3].wait()
    pair[1].wait_recv()
    prepare(0)

    pair[2].wait_recv()
    for b in range(3):
        q = pl.multiple_of(256 * jnp.where(c == 0, b, 3 - b), 256)
        wet_b = jnp.broadcast_to(wet[:, pl.ds(q, 256)], (32, 256)).astype(F32).astype(BF)
        x_1 = xo[1, :, pl.ds(q, 256)]
        x_o = jnp.concatenate(
            [xo[0, :, pl.ds(q, 256)], x_1] + [x_1[48:80]] * 2 + [wet_b], axis=0
        )
        v_o = lax.dot_general(tsel[b], x_o, NT, preferred_element_type=F32)
        for il in range(8):
            i = 8 * b + il
            rows = slice(32 * il, 32 * il + 32)
            for g in [STRIDE * (i + 1) + 16] + ([16] if i == 0 else []):
                if i <= 16:
                    oc_a[g : g + 32] = v_o[rows, :128]
                    oc_b[g : g + 32] = v_o[rows, 128:]

    for n in (1, 2):
        loads[3 + n].wait()
        pair[2 + n].wait_recv()
        prepare(n)
    loads[6].wait()
    loads[7].wait()

    for d in range(2):
        for sender in range(2):
            pltpu.make_async_remote_copy(
                src_ref=sbuf.at[0, d],
                dst_ref=halo.at[sender, :, pl.ds(128 * d, 128)],
                send_sem=hsem_s.at[0],
                recv_sem=hsem_r.at[d, sender],
                device_id=partner,
                device_id_type=MESH,
            ).wait_recv()
    h_1 = halo[1, 48:80]
    h_atm = jnp.concatenate([halo[0, 0:80], halo[1, 0:80]] + [h_1] * 3, axis=0)
    h_oc = jnp.concatenate(
        [halo[0, 0:80], halo[1, 0:80]] + [h_1] * 2 + [halo[0, 80:96]] * 2, axis=0
    )
    v_a = lax.dot_general(hsel[...], h_atm, NT, preferred_element_type=F32)
    v_o = lax.dot_general(osel[...], h_oc, NT, preferred_element_type=F32)
    for k in range(23):
        rows = slice(16 * k, 16 * k + 16)
        g = STRIDE * k
        st_a[g : g + 16] = v_a[rows, :128]
        st_b[g : g + 16] = v_a[rows, 128:]
        put(0, g, *normed(v_a[rows, :128], v_a[rows, 128:], gain_a, gain_b), rows=16)
        if k < 19:
            oc_a[g : g + 16] = v_o[rows, :128]
            oc_b[g : g + 16] = v_o[rows, 128:]

    group = lax.shift_right_logical(iota((1, 128), 1), 5)

    def bounds(n):
        cuts = list(range(0, n, GROUP))
        if n - cuts[-1] < GROUP // 2:
            cuts.pop()
        return list(zip(cuts, cuts[1:] + [n]))

    def products(v, n, wi, lo, hi):
        a = 48 if lo == 0 else STRIDE * lo + 64
        z = STRIDE * hi + 64
        lhs = jnp.concatenate(
            [va[v, a - 48 : z - 48], va[v, a:z], va[v, a + 48 : z + 48], bc[v, a + 48 : z + 48]],
            axis=1,
        )
        pbuf[a:z] = lax.dot_general(lhs, wb[wi], NT, preferred_element_type=F32)

    def finish(v, n, epilogue, lo, hi):
        def piece(m, g, rows):
            x = pbuf[pl.ds(g - 8, rows + 16)]
            mid = slice(8, 8 + rows)
            p_b = x[:, 384:512]
            out_a = (
                x[mid, 128:256]
                + pltpu.roll(x[:, 0:128], 1, 0)[mid]
                + pltpu.roll(x[:, 256:384], rows + 15, 0)[mid]
            )
            y = jnp.where(group == 0, pltpu.roll(p_b, 1, 0)[mid], 0.0)
            y = jnp.where(group == 1, p_b[mid], y)
            y = jnp.where(group == 2, pltpu.roll(p_b, rows + 15, 0)[mid], y)
            y = y + pltpu.roll(y, 64, 1)
            epilogue(v, m, g, rows, out_a, y + pltpu.roll(y, 32, 1))

        @pl.loop(lo, hi, unroll=True)
        def _(m):
            piece(m, pl.multiple_of(STRIDE * m + STRIDE, STRIDE), STRIDE)

        if hi == n and n > 16:
            piece(n, STRIDE * n + STRIDE, 16)

    def replicate(v):
        first = iota((16, 128), 0) < 8

        def mix(own, nxt):
            mask = first[:, : own.shape[1]]
            return jnp.where(mask, nxt.astype(F32), own.astype(F32)).astype(BF)

        for ref, at, lanes in (
            (va, 0, slice(0, 128)),
            (bc, 96, slice(0, 32)),
            (bc, 48, slice(32, 64)),
            (bc, 0, slice(64, 96)),
        ):
            own, nxt = ref[v, at + 48 : at + 64, lanes], ref[v, at + 96 : at + 112, lanes]
            ref[v, at : at + 16, lanes] = own
            ref[v, at + 16 : at + 48, lanes] = ref[v, at + 64 : at + 96, lanes]
            ref[v, at + 48 : at + 64, lanes] = mix(own, nxt)

    def gelu(x):
        return jax.nn.gelu(x, approximate=True)

    def hidden(v, m, g, rows, o_a, o_b):
        put(v, g, gelu(o_a), gelu(o_b), rows)

    def first_state(v, m, g, rows, o_a, o_b):
        s_a = (st_a[pl.ds(g, rows)] + o_a).astype(BF).astype(F32)
        s_b = (st_b[pl.ds(g, rows)] + o_b).astype(BF).astype(F32)
        st_a[pl.ds(g, rows)] = s_a
        st_b[pl.ds(g, rows)] = s_b
        put(v, g, *normed(s_a, s_b, gain_a, gain_b), rows)

    def second_state(v, m, g, rows, o_a, o_b):
        s_a, s_b = st_a[pl.ds(g, rows)], st_b[pl.ds(g, rows)]
        t_a = (s_a + o_a).astype(BF)
        t_b = (s_b + o_b).astype(BF)
        if rows == STRIDE:
            r = pl.multiple_of(32 * m, 32)
            fin[0, pl.ds(r, 32), 0:128] = t_a[16:48]
            fin[0, pl.ds(r, 32), 128:256] = t_b[16:48]
        y_a, y_b = oc_a[pl.ds(g, rows)], oc_b[pl.ds(g, rows)]
        mask = y_b[:, 96:97]
        put(
            v,
            g,
            (y_a + 0.5 * (s_a + t_a.astype(F32))) * mask,
            (y_b + 0.5 * (s_b + t_b.astype(F32))) * mask,
            rows,
        )

    def mixed(v, m, g, rows, o_a, o_b):
        n_a, n_b = normed(
            o_a.astype(BF).astype(F32), o_b.astype(BF).astype(F32), ocean_a, ocean_b
        )
        r = pl.multiple_of(32 * m, 32)
        nrm[pl.ds(r, 32), 0:128] = n_a[16:48].astype(BF)
        nrm[pl.ds(r, 32), 128:256] = n_b[16:48].astype(BF)

    outs = []

    def send_out(n, k, src, dst):
        copy = pltpu.make_async_remote_copy(
            src_ref=src,
            dst_ref=dst,
            send_sem=osem_s.at[k],
            recv_sem=osem_r.at[k],
            device_id=partner,
            device_id_type=MESH,
        )
        copy.start()
        outs.append(copy)

    mine = pl.ds(pl.multiple_of(512 * c, 512), 512)

    def stored(n, b):
        return lax.dot_general(
            fin[n, 256 * b : 256 * b + 256][:, :160], tsel[b], TN, preferred_element_type=F32
        )

    def atmosphere_out():
        for b in range(2):
            o = pl.multiple_of(256 * jnp.where(c == 0, b, 1 - b), 256)
            t_a = stored(0, b).astype(BF)
            for k in range(2):
                obuf[0, k, :, pl.ds(o, 256)] = t_a[80 * k : 80 * k + 80]
        send_out(0, 0, obuf.at[0, pc], out_a.at[:, mine])
        out_a[:, mine] = obuf[0, c]

    def ocean_out(b):
        h = jnp.dot(
            nrm[256 * b : 256 * b + 256, :][:, :160], miv[...], preferred_element_type=F32
        )
        h = gelu(h).astype(BF)
        u = lax.dot_general(h, mov[...], NT, preferred_element_type=F32).astype(BF)
        fin[1, 256 * b : 256 * b + 256, 0:160] = u
        q = pl.multiple_of(256 * jnp.where(c == 0, b, 3 - b), 256)
        o = pl.multiple_of(256 * jnp.where(c == 0, b, 1 - b), 256)
        u = stored(1, b)
        w_row = wet[:, pl.ds(q, 256)].astype(F32)
        for k in range(2):
            obuf[1, k, :, pl.ds(o, 256)] = (
                xo[k, :, pl.ds(q, 256)].astype(F32) + w_row * u[80 * k : 80 * k + 80]
            ).astype(BF)
        here = pl.ds(pl.multiple_of(512 * c + o, 256), 256)
        send_out(1, 1 + b, obuf.at[1, pc, :, pl.ds(o, 256)], out_o.at[:, here])
        out_o[:, here] = obuf[1, c, :, pl.ds(o, 256)]

    steps = []
    for k, (n, wi, epilogue) in enumerate(
        ((20, 0, hidden), (19, 1, first_state), (18, 0, hidden), (17, 1, second_state), (16, 2, mixed))
    ):
        for i, (lo, hi) in enumerate(bounds(n)):
            steps.append((k, n, wi, epilogue, i, lo, hi))
    ready = 0
    for at, (k, n, wi, epilogue, i, lo, hi) in enumerate(steps):
        while ready < min(at + AHEAD, len(steps)):
            d = steps[ready]
            if d[0] > k:
                done = steps[at - 1] if at else None
                need = min(d[6] + 2, d[1] + 1)
                if d[0] > k + 1 or done is None or done[0] < k or done[6] < min(need, n):
                    break
            products(d[0] % 2, d[1], d[2], d[5], d[6])
            ready += 1
        finish(1 - k % 2, n, epilogue, lo, hi)
        if i == 0 and k < 4:
            replicate(1 - k % 2)
        if k == 4 and i == 0:
            atmosphere_out()
        if k == 4 and hi >= 8 and lo < 8:
            ocean_out(0)
    ocean_out(1)

    for copy in halo_copies:
        copy.wait_send()
    for copy in pair:
        copy.wait_send()
    for copy in outs:
        copy.wait()


def write_out(a, o, out_a, out_o, sem):
    copies = [
        pltpu.make_async_copy(a, out_a, sem.at[0]),
        pltpu.make_async_copy(o, out_o, sem.at[1]),
    ]
    for copy in copies:
        copy.start()
    for copy in copies:
        copy.wait()


def per_device(
    atm_state, ocean_state, wet_mask, neighbours, west_rim, east_rim, atm_gain,
    atm_conv_in, atm_conv_out, ocean_conv, ocean_gain, mlp_in, mlp_out,
):
    vmem = pl.BlockSpec(memory_space=pltpu.VMEM)
    anym = pl.BlockSpec(memory_space=pl.ANY)
    hbm = pl.BlockSpec(memory_space=pltpu.HBM)
    pixels = atm_state.shape[1]
    pin = lambda x: pltpu.with_memory_space_constraint(x, pltpu.HBM)
    taps = [pin(jnp.transpose(w, (1, 0, 2))) for w in (atm_conv_in, atm_conv_out, ocean_conv)]
    out = jax.ShapeDtypeStruct((CH, pixels), BF)
    dma = pltpu.SemaphoreType.DMA
    parts = pl.pallas_call(
        kernel,
        name="coupled_step",
        out_shape=(out, out),
        in_specs=[anym] * 11,
        out_specs=(vmem, vmem),
        scratch_shapes=[
            pltpu.VMEM((2, CH, pixels), BF),
            pltpu.VMEM((2, CH, pixels), BF),
            pltpu.VMEM((3, 2, 9, CH, C), BF),
            pltpu.VMEM((3, 512, 512), BF),
            pltpu.VMEM((C, 640), BF),
            pltpu.VMEM((C, 640), BF),
            pltpu.VMEM((2, 8, pixels), jnp.int32),
            pltpu.VMEM((3, 256, 256), BF),
            pltpu.VMEM((2, 2, 96, 128), BF),
            pltpu.VMEM((2, 96, 256), BF),
            pltpu.VMEM((BUF, 128), F32),
            pltpu.VMEM((BUF, 128), F32),
            pltpu.VMEM((BUF, 128), F32),
            pltpu.VMEM((BUF, 128), F32),
            pltpu.VMEM((2, BUF, 128), BF),
            pltpu.VMEM((2, BC, 128), BF),
            pltpu.VMEM((BUF, 512), F32),
            pltpu.VMEM((576, 256), BF),
            pltpu.VMEM((2, 576, 256), BF),
            pltpu.VMEM((2, 2, CH, 512), BF),
            pltpu.VMEM((8, pixels), jnp.int32),
            pltpu.VMEM((1, pixels), jnp.int32),
            pltpu.VMEM((1, C), F32),
            pltpu.VMEM((1, C), F32),
            pltpu.VMEM((368, 256), BF),
            pltpu.VMEM((304, 256), BF),
            dma((11,)),
            dma((5,)),
            dma((5,)),
            dma((4,)),
            dma((2, 2)),
            dma((3,)),
            dma((3,)),
        ],
        compiler_params=pltpu.CompilerParams(
            collective_id=0, has_side_effects=True, vmem_limit_bytes=48 * 1024 * 1024
        ),
    )(
        pin(neighbours),
        pin(wet_mask.reshape(1, pixels)),
        pin(atm_gain.reshape(1, C)),
        pin(ocean_gain.reshape(1, C)),
        pin(atm_state),
        pin(ocean_state),
        *taps,
        pin(jnp.transpose(mlp_in)),
        pin(mlp_out),
    )
    return pl.pallas_call(
        write_out,
        name="write_out",
        out_shape=(out, out),
        in_specs=[vmem] * 2,
        out_specs=(hbm, hbm),
        scratch_shapes=[dma((2,))],
    )(*[pltpu.with_memory_space_constraint(x, pltpu.VMEM) for x in parts])


def solution(mesh):
    in_specs = (
        P("chan", "sector"),
        P("chan", "sector"),
        P("sector"),
        P(None, "sector"),
        P("sector"),
        P("sector"),
        P(),
        P("chan", None, None),
        P("chan", None, None),
        P("chan", None, None),
        P(),
        P(),
        P(),
    )
    out_specs = (P("chan", "sector"), P("chan", "sector"))
    return jax.shard_map(
        per_device, mesh=mesh, in_specs=in_specs, out_specs=out_specs, check_vma=False
    )
```

```python
import functools

import jax
import jax.numpy as jnp
from jax import lax
from jax.experimental import pallas as pl
from jax.experimental.pallas import tpu as pltpu
from jax.sharding import PartitionSpec as P

EPSILON = 1e-06
CH = 80
C = 160
ROWS = 32
STRIDE = 48
BUF = 1104
BC = BUF + 96
GROUP = 10
AHEAD = 2
MESH = pl.DeviceIdType.MESH
NT = (((1,), (1,)), ((), ()))
TN = (((0,), (0,)), ((), ()))
F32 = jnp.float32
BF = jnp.bfloat16


def iota(shape, dim):
    return lax.broadcasted_iota(jnp.int32, shape, dim)


def onehot(hit):
    return jnp.where(hit, 1.0, 0.0).astype(BF)


def kernel(
    nb, wet_h, ga_h, go_h, atm, oc, w1, w2, w3, mi, mo,
    out_a, out_o,
    xa, xo, wraw_0, wraw_1, wraw_2, wb, miv, mov, keys, tsel, sbuf, halo, st_a, st_b, oc_a, oc_b,
    va, bc, pbuf, nrm, fin, obuf, nbv, wet, ga, go, hsel, osel,
    lsem, psem_s, psem_r, hsem_s, hsem_r, osem_s, osem_r,
):
    wraw = (wraw_0, wraw_1, wraw_2)
    sectors = lax.axis_size("sector")
    s = lax.axis_index("sector")
    c = lax.axis_index("chan")
    pc = 1 - c
    west = lax.rem(s + sectors - 1, sectors)
    east = lax.rem(s + 1, sectors)
    partner = {"sector": s, "chan": pc}

    bar = pltpu.get_barrier_semaphore()
    pl.semaphore_signal(bar, inc=1, device_id=partner, device_id_type=MESH)
    for chip in (west, east):
        for t in range(2):
            pl.semaphore_signal(
                bar, inc=1, device_id={"sector": chip, "chan": t}, device_id_type=MESH
            )

    loads = [
        pltpu.make_async_copy(nb, nbv, lsem.at[0]),
        pltpu.make_async_copy(atm, xa.at[c], lsem.at[1]),
        pltpu.make_async_copy(oc, xo.at[c], lsem.at[2]),
        pltpu.make_async_copy(w1, wraw[0].at[c], lsem.at[3]),
        pltpu.make_async_copy(w2, wraw[1].at[c], lsem.at[4]),
        pltpu.make_async_copy(w3, wraw[2].at[c], lsem.at[5]),
        pltpu.make_async_copy(mi, miv, lsem.at[6]),
        pltpu.make_async_copy(mo, mov, lsem.at[7]),
        pltpu.make_async_copy(wet_h, wet, lsem.at[8]),
        pltpu.make_async_copy(ga_h, ga, lsem.at[9]),
        pltpu.make_async_copy(go_h, go, lsem.at[10]),
    ]
    for n in (0, 1, 2, 8):
        loads[n].start()
    loads[0].wait()

    v = nbv[:, 0:128]
    lane = iota((8, 128), 1)
    sample = lax.shift_right_logical(lane, 5) == 1
    beyond = v >= 1024
    cycle = jnp.where(beyond, v & 31, lax.shift_right_logical(v, 5))
    side = jnp.where(beyond, jnp.where(v < 1056, 1, 2), 0)
    code = jnp.max(jnp.where(sample, 4 * cycle + side, 0), axis=1, keepdims=True)
    side = code & 3
    towards = 3 * lax.shift_right_logical(code, 2) + jnp.where(side == 0, 1, 2 * side - 2)

    for b in range(8):
        v = jnp.where(towards == 3, nbv[:, 128 * b : 128 * b + 128], 0)
        v = jnp.broadcast_to(jnp.max(v, axis=0, keepdims=True), (8, 128))
        inside = v < 1024
        hop = jnp.where(inside, v - 128 * b, lane)
        col = jnp.where(inside, 1, 0)
        for _ in range(5):
            col = col + jnp.take_along_axis(col, hop, axis=1, mode="promise_in_bounds")
            hop = jnp.take_along_axis(hop, hop, axis=1, mode="promise_in_bounds")
        cyc = 4 * b + lax.shift_right_logical(lane, 5)
        keys[0, :, 128 * b : 128 * b + 128] = 32 * cyc + col
        keys[1, :, 128 * b : 128 * b + 128] = 32 * (31 - cyc) + col

    loads[1].wait()
    loads[2].wait()
    loads[8].wait()

    wet16 = jnp.broadcast_to(wet[...], (16, 1024)).astype(F32).astype(BF)

    hr = iota((256, 256), 0)
    hh = hr & 127
    far = hr >= 128
    hi = lax.shift_right_logical(hh * 205, 10)
    he = hh - 5 * hi
    key_a = jnp.where(hh < 105, 32 * hi + jnp.where(far, 27 + he, he), -1)
    key_o = jnp.where(
        (hh >= 105) & (hh < 122), 32 * (hh - 105) + jnp.where(far, 31, 0), -1
    )
    z16 = jnp.zeros((16, 256), BF)

    def picked(keys_h, key_q, lo, hi):
        parts = []
        for d in (0, 128):
            rows = slice(d + lo, d + hi)
            if lo:
                parts.append(jnp.zeros((lo, 256), BF))
            parts.append(onehot(keys_h[rows] == key_q))
            if hi < 128:
                parts.append(jnp.zeros((128 - hi, 256), BF))
        return jnp.concatenate(parts, axis=0)

    for t in range(2):
        total = jnp.zeros((96, 256), F32)
        for b in range(3):
            q = 256 * (b if t == 0 else 3 - b)
            key_q = keys[t, 0:1, q : q + 256]
            x_a = jnp.concatenate([xa[c, :, q : q + 256], z16], axis=0)
            x_o = jnp.concatenate([xo[c, :, q : q + 256], wet16[:, q : q + 256]], axis=0)
            total = total + lax.dot_general(
                x_a, picked(key_a, key_q, *((0, 48), (32, 80), (80, 112))[b]), NT, preferred_element_type=F32
            )
            total = total + lax.dot_general(
                x_o, picked(key_o, key_q, 96, 128), NT, preferred_element_type=F32
            )
        sbuf[t, 0] = total[:, :128].astype(BF)
        sbuf[t, 1] = total[:, 128:].astype(BF)

    pl.semaphore_wait(bar, 5)

    halo_copies = []
    for t in range(2):
        for d, chip in ((0, west), (1, east)):
            halo_copies.append(
                pltpu.make_async_remote_copy(
                    src_ref=sbuf.at[t, d],
                    dst_ref=halo.at[c, :, pl.ds(128 * d, 128)],
                    send_sem=hsem_s.at[2 * t + d],
                    recv_sem=hsem_r.at[d, c],
                    device_id={"sector": chip, "chan": t},
                    device_id_type=MESH,
                )
            )
    for copy in halo_copies:
        copy.start()

    def to_partner(src, dst, n):
        return pltpu.make_async_remote_copy(
            src_ref=src,
            dst_ref=dst,
            send_sem=psem_s.at[n],
            recv_sem=psem_r.at[n],
            device_id=partner,
            device_id_type=MESH,
        )

    window = pl.ds(pl.multiple_of(256 * pc, 256), 768)
    pair = [
        to_partner(atm.at[:, window], xa.at[c, :, window], 0),
        to_partner(w1, wraw[0].at[c], 1),
        to_partner(oc.at[:, window], xo.at[c, :, window], 2),
        to_partner(w2, wraw[1].at[c], 3),
        to_partner(w3, wraw[2].at[c], 4),
    ]
    for copy in pair:
        copy.start()
    for n in (3, 9, 10, 4, 5, 6, 7):
        loads[n].start()

    for b in range(3):
        q = pl.multiple_of(256 * jnp.where(c == 0, b, 3 - b), 256)
        key_q = keys[c, 0:1, pl.ds(q, 256)] - 256 * b
        tsel[b] = onehot(iota((256, 256), 0) == key_q)

    slots = [
        jnp.max(jnp.where(towards == m, iota((8, 1), 0) + 1, 0)) if m != 4 else 0
        for m in range(9)
    ]

    def prepare(n):
        wb[n, :, 480:512] = jnp.zeros((512, 32), BF)
        wb[n, 480:512, :] = jnp.zeros((32, 512), BF)
        for dyi in range(3):
            for dxi in range(3):
                k = jnp.where(c == 0, slots[3 * dyi + dxi], slots[3 * (2 - dyi) + dxi])
                w_0 = wraw[n][0, k]
                w_1 = wraw[n][1, k]
                for lanes, dst, width in (
                    (slice(0, 128), 128 * dyi, 128),
                    (slice(128, 160), 384 + 32 * dyi, 32),
                ):
                    r = 128 * dxi
                    wb[n, r : r + 80, dst : dst + width] = w_0[:, lanes]
                    wb[n, r + 80 : r + 128, dst : dst + width] = w_1[0:48, lanes]
                    r = 384 + 32 * dxi
                    wb[n, r : r + 32, dst : dst + width] = w_1[48:80, lanes]

    hl = iota((1, 256), 1)
    hh = hl & 127
    far = hl >= 128
    hi = lax.shift_right_logical(hh * 205, 10)
    he = hh - 5 * hi
    p1 = jnp.where(hh < 105, jnp.where(far, 16 * hi + 27 + he, 16 * hi + 32 + he), -1)
    p2 = jnp.where(hi == 0, p1 - 16, p1)
    r = iota((368, 256), 0)
    hsel[...] = onehot((r == p1) | (r == p2))
    oi = hh - 105
    p1 = jnp.where((oi >= 0) & (oi < 17), jnp.where(far, 16 * oi + 31, 16 * oi + 32), -1)
    p2 = jnp.where(oi == 0, p1 - 16, p1)
    r = iota((304, 256), 0)
    osel[...] = onehot((r == p1) | (r == p2))

    loads[9].wait()
    loads[10].wait()
    gain_a = ga[:, 0:128]
    gain_b = jnp.concatenate([ga[:, 128:160]] * 4, axis=1)
    ocean_a = go[:, 0:128]
    ocean_b = jnp.concatenate([go[:, 128:160]] * 4, axis=1)

    def normed(x_a, x_b, scale_a, scale_b):
        mean_sq = jnp.sum(x_a * x_a + 0.25 * (x_b * x_b), axis=1, keepdims=True) * (1.0 / C)
        inv = lax.rsqrt(mean_sq + EPSILON)
        return x_a * inv * scale_a, x_b * inv * scale_b

    def put(v, g, x_a, x_b, rows=STRIDE):
        va[v, pl.ds(g, rows)] = x_a.astype(BF)
        y = x_b.astype(BF)
        bc[v, pl.ds(g + 2 * STRIDE, rows), 0:32] = y[:, 0:32]
        bc[v, pl.ds(g + STRIDE, rows), 32:64] = y[:, 32:64]
        bc[v, pl.ds(g, rows), 64:96] = y[:, 64:96]

    for v in range(2):
        bc[v, :, 96:128] = jnp.zeros((BC, 32), BF)

    pair[0].wait_recv()
    for b in range(3):
        q = pl.multiple_of(256 * jnp.where(c == 0, b, 3 - b), 256)
        x_1 = xa[1, :, pl.ds(q, 256)]
        x_a = jnp.concatenate([xa[0, :, pl.ds(q, 256)], x_1] + [x_1[48:80]] * 3, axis=0)
        v_a = lax.dot_general(tsel[b], x_a, NT, preferred_element_type=F32)
        for il in range(8):
            i = 8 * b + il
            rows = slice(32 * il, 32 * il + 32)
            if i <= 20:
                n_a, n_b = normed(v_a[rows, :128], v_a[rows, 128:], gain_a, gain_b)
            for g in [STRIDE * (i + 1) + 16] + ([16] if i == 0 else []):
                if i <= 20:
                    st_a[g : g + 32] = v_a[rows, :128]
                    st_b[g : g + 32] = v_a[rows, 128:]
                    put(0, g, n_a, n_b, rows=32)

    loads[3].wait()
    pair[1].wait_recv()
    prepare(0)

    pair[2].wait_recv()
    for b in range(3):
        q = pl.multiple_of(256 * jnp.where(c == 0, b, 3 - b), 256)
        wet_b = jnp.broadcast_to(wet[:, pl.ds(q, 256)], (32, 256)).astype(F32).astype(BF)
        x_1 = xo[1, :, pl.ds(q, 256)]
        x_o = jnp.concatenate(
            [xo[0, :, pl.ds(q, 256)], x_1] + [x_1[48:80]] * 2 + [wet_b], axis=0
        )
        v_o = lax.dot_general(tsel[b], x_o, NT, preferred_element_type=F32)
        for il in range(8):
            i = 8 * b + il
            rows = slice(32 * il, 32 * il + 32)
            for g in [STRIDE * (i + 1) + 16] + ([16] if i == 0 else []):
                if i <= 16:
                    oc_a[g : g + 32] = v_o[rows, :128]
                    oc_b[g : g + 32] = v_o[rows, 128:]

    for n in (1, 2):
        loads[3 + n].wait()
        pair[2 + n].wait_recv()
        prepare(n)
    loads[6].wait()
    loads[7].wait()

    for d in range(2):
        for sender in range(2):
            pltpu.make_async_remote_copy(
                src_ref=sbuf.at[0, d],
                dst_ref=halo.at[sender, :, pl.ds(128 * d, 128)],
                send_sem=hsem_s.at[0],
                recv_sem=hsem_r.at[d, sender],
                device_id=partner,
                device_id_type=MESH,
            ).wait_recv()
    h_1 = halo[1, 48:80]
    h_atm = jnp.concatenate([halo[0, 0:80], halo[1, 0:80]] + [h_1] * 3, axis=0)
    h_oc = jnp.concatenate(
        [halo[0, 0:80], halo[1, 0:80]] + [h_1] * 2 + [halo[0, 80:96]] * 2, axis=0
    )
    v_a = lax.dot_general(hsel[...], h_atm, NT, preferred_element_type=F32)
    for k in range(23):
        rows = slice(16 * k, 16 * k + 16)
        g = STRIDE * k
        st_a[g : g + 16] = v_a[rows, :128]
        st_b[g : g + 16] = v_a[rows, 128:]
        put(0, g, *normed(v_a[rows, :128], v_a[rows, 128:], gain_a, gain_b), rows=16)
    v_o = lax.dot_general(osel[...], h_oc, NT, preferred_element_type=F32)
    for k in range(19):
        rows = slice(16 * k, 16 * k + 16)
        g = STRIDE * k
        oc_a[g : g + 16] = v_o[rows, :128]
        oc_b[g : g + 16] = v_o[rows, 128:]

    group = lax.shift_right_logical(iota((1, 128), 1), 5)

    def bounds(n):
        cuts = list(range(0, n, GROUP))
        if n - cuts[-1] < GROUP // 2:
            cuts.pop()
        return list(zip(cuts, cuts[1:] + [n]))

    def products(v, n, wi, lo, hi):
        a = 48 if lo == 0 else STRIDE * lo + 64
        z = STRIDE * hi + 64
        lhs = jnp.concatenate(
            [va[v, a - 48 : z - 48], va[v, a:z], va[v, a + 48 : z + 48], bc[v, a + 48 : z + 48]],
            axis=1,
        )
        pbuf[a:z] = lax.dot_general(lhs, wb[wi], NT, preferred_element_type=F32)

    def finish(v, n, epilogue, lo, hi):
        def piece(m, g, rows):
            x = pbuf[pl.ds(g - 8, rows + 16)]
            mid = slice(8, 8 + rows)
            p_b = x[:, 384:512]
            out_a = (
                x[mid, 128:256]
                + pltpu.roll(x[:, 0:128], 1, 0)[mid]
                + pltpu.roll(x[:, 256:384], rows + 15, 0)[mid]
            )
            y = jnp.where(group == 0, pltpu.roll(p_b, 1, 0)[mid], 0.0)
            y = jnp.where(group == 1, p_b[mid], y)
            y = jnp.where(group == 2, pltpu.roll(p_b, rows + 15, 0)[mid], y)
            y = y + pltpu.roll(y, 64, 1)
            epilogue(v, m, g, rows, out_a, y + pltpu.roll(y, 32, 1))

        @pl.loop(lo, hi, unroll=True)
        def _(m):
            if n > 16:
                piece(m, pl.multiple_of(STRIDE * m + STRIDE, STRIDE), STRIDE)
            else:
                piece(m, pl.multiple_of(STRIDE * m + STRIDE + 16, 16), 32)

        if hi == n and n > 16:
            piece(n, STRIDE * n + STRIDE, 16)

    def replicate(v):
        first = iota((16, 128), 0) < 8

        def mix(own, nxt):
            mask = first[:, : own.shape[1]]
            return jnp.where(mask, nxt.astype(F32), own.astype(F32)).astype(BF)

        for ref, at, lanes in (
            (va, 0, slice(0, 128)),
            (bc, 96, slice(0, 32)),
            (bc, 48, slice(32, 64)),
            (bc, 0, slice(64, 96)),
        ):
            own, nxt = ref[v, at + 48 : at + 64, lanes], ref[v, at + 96 : at + 112, lanes]
            ref[v, at : at + 16, lanes] = own
            ref[v, at + 16 : at + 48, lanes] = ref[v, at + 64 : at + 96, lanes]
            ref[v, at + 48 : at + 64, lanes] = mix(own, nxt)

    def gelu(x):
        half = 0.5 * x
        return half + half * jnp.tanh(x * (0.7978845608028654 + 0.035677408136300125 * (x * x)))

    def hidden(v, m, g, rows, o_a, o_b):
        put(v, g, gelu(o_a), gelu(o_b), rows)

    def first_state(v, m, g, rows, o_a, o_b):
        s_a = (st_a[pl.ds(g, rows)] + o_a).astype(BF).astype(F32)
        s_b = (st_b[pl.ds(g, rows)] + o_b).astype(BF).astype(F32)
        st_a[pl.ds(g, rows)] = s_a
        st_b[pl.ds(g, rows)] = s_b
        put(v, g, *normed(s_a, s_b, gain_a, gain_b), rows)

    def second_state(v, m, g, rows, o_a, o_b):
        s_a, s_b = st_a[pl.ds(g, rows)], st_b[pl.ds(g, rows)]
        t_a = (s_a + o_a).astype(BF)
        t_b = (s_b + o_b).astype(BF)
        if rows == STRIDE:
            r = pl.multiple_of(32 * m, 32)
            fin[0, pl.ds(r, 32), 0:128] = t_a[16:48]
            fin[0, pl.ds(r, 32), 128:256] = t_b[16:48]
        y_a, y_b = oc_a[pl.ds(g, rows)], oc_b[pl.ds(g, rows)]
        mask = y_b[:, 96:97]
        put(
            v,
            g,
            (y_a + 0.5 * (s_a + t_a.astype(F32))) * mask,
            (y_b + 0.5 * (s_b + t_b.astype(F32))) * mask,
            rows,
        )

    def mixed(v, m, g, rows, o_a, o_b):
        n_a, n_b = normed(
            o_a.astype(BF).astype(F32), o_b.astype(BF).astype(F32), ocean_a, ocean_b
        )
        r = pl.multiple_of(32 * m, 32)
        nrm[pl.ds(r, 32), 0:128] = n_a.astype(BF)
        nrm[pl.ds(r, 32), 128:256] = n_b.astype(BF)

    outs = []

    def send_out(n, k, src, dst):
        copy = pltpu.make_async_remote_copy(
            src_ref=src,
            dst_ref=dst,
            send_sem=osem_s.at[k],
            recv_sem=osem_r.at[k],
            device_id=partner,
            device_id_type=MESH,
        )
        copy.start()
        outs.append(copy)

    mine = pl.ds(pl.multiple_of(512 * c, 512), 512)

    def stored(n, b):
        return lax.dot_general(
            fin[n, 256 * b : 256 * b + 256][:, :160], tsel[b], TN, preferred_element_type=F32
        )

    def atmosphere_out():
        for b in range(2):
            o = pl.multiple_of(256 * jnp.where(c == 0, b, 1 - b), 256)
            t_a = stored(0, b).astype(BF)
            for k in range(2):
                obuf[0, k, :, pl.ds(o, 256)] = t_a[80 * k : 80 * k + 80]
        send_out(0, 0, obuf.at[0, pc], out_a.at[:, mine])
        out_a[:, mine] = obuf[0, c]

    def ocean_out(b):
        h = jnp.dot(
            nrm[256 * b : 256 * b + 256, :][:, :160], miv[...], preferred_element_type=F32
        )
        h = gelu(h).astype(BF)
        u = lax.dot_general(mov[...], h, NT, preferred_element_type=F32).astype(BF)
        q = pl.multiple_of(256 * jnp.where(c == 0, b, 3 - b), 256)
        o = pl.multiple_of(256 * jnp.where(c == 0, b, 1 - b), 256)
        u = jnp.dot(u, tsel[b], preferred_element_type=F32)
        w_row = wet[:, pl.ds(q, 256)].astype(F32)
        for k in range(2):
            obuf[1, k, :, pl.ds(o, 256)] = (
                xo[k, :, pl.ds(q, 256)].astype(F32) + w_row * u[80 * k : 80 * k + 80]
            ).astype(BF)
        here = pl.ds(pl.multiple_of(512 * c + o, 256), 256)
        send_out(1, 1 + b, obuf.at[1, pc, :, pl.ds(o, 256)], out_o.at[:, here])
        out_o[:, here] = obuf[1, c, :, pl.ds(o, 256)]

    steps = []
    for k, (n, wi, epilogue) in enumerate(
        ((20, 0, hidden), (19, 1, first_state), (18, 0, hidden), (17, 1, second_state), (16, 2, mixed))
    ):
        for i, (lo, hi) in enumerate(bounds(n)):
            steps.append((k, n, wi, epilogue, i, lo, hi))
    ready = 0
    for at, (k, n, wi, epilogue, i, lo, hi) in enumerate(steps):
        while ready < min(at + AHEAD, len(steps)):
            d = steps[ready]
            if d[0] > k:
                done = steps[at - 1] if at else None
                need = min(d[6] + 2, d[1] + 1)
                if d[0] > k + 1 or done is None or done[0] < k or done[6] < min(need, n):
                    break
            products(d[0] % 2, d[1], d[2], d[5], d[6])
            ready += 1
        finish(1 - k % 2, n, epilogue, lo, hi)
        if i == 0 and k < 4:
            replicate(1 - k % 2)
        if k == 4 and i == 0:
            atmosphere_out()
        if k == 4 and hi >= 8 and lo < 8:
            ocean_out(0)
    ocean_out(1)

    for copy in halo_copies:
        copy.wait_send()
    for copy in pair:
        copy.wait_send()
    for copy in outs:
        copy.wait()


def write_out(a, o, out_a, out_o, sem):
    copies = [
        pltpu.make_async_copy(a, out_a, sem.at[0]),
        pltpu.make_async_copy(o, out_o, sem.at[1]),
    ]
    for copy in copies:
        copy.start()
    for copy in copies:
        copy.wait()


def per_device(
    atm_state, ocean_state, wet_mask, neighbours, west_rim, east_rim, atm_gain,
    atm_conv_in, atm_conv_out, ocean_conv, ocean_gain, mlp_in, mlp_out,
):
    vmem = pl.BlockSpec(memory_space=pltpu.VMEM)
    anym = pl.BlockSpec(memory_space=pl.ANY)
    hbm = pl.BlockSpec(memory_space=pltpu.HBM)
    pixels = atm_state.shape[1]
    pin = lambda x: pltpu.with_memory_space_constraint(x, pltpu.HBM)
    taps = [pin(jnp.transpose(w, (1, 0, 2))) for w in (atm_conv_in, atm_conv_out, ocean_conv)]
    out = jax.ShapeDtypeStruct((CH, pixels), BF)
    dma = pltpu.SemaphoreType.DMA
    parts = pl.pallas_call(
        kernel,
        name="coupled_step",
        out_shape=(out, out),
        in_specs=[anym] * 11,
        out_specs=(vmem, vmem),
        scratch_shapes=[
            pltpu.VMEM((2, CH, pixels), BF),
            pltpu.VMEM((2, CH, pixels), BF),
            pltpu.VMEM((2, 9, CH, C), BF),
            pltpu.VMEM((2, 9, CH, C), BF),
            pltpu.VMEM((2, 9, CH, C), BF),
            pltpu.VMEM((3, 512, 512), BF),
            pltpu.VMEM((C, 640), BF),
            pltpu.VMEM((C, 640), BF),
            pltpu.VMEM((2, 8, pixels), jnp.int32),
            pltpu.VMEM((3, 256, 256), BF),
            pltpu.VMEM((2, 2, 96, 128), BF),
            pltpu.VMEM((2, 96, 256), BF),
            pltpu.VMEM((BUF, 128), F32),
            pltpu.VMEM((BUF, 128), F32),
            pltpu.VMEM((BUF, 128), F32),
            pltpu.VMEM((BUF, 128), F32),
            pltpu.VMEM((2, BUF, 128), BF),
            pltpu.VMEM((2, BC, 128), BF),
            pltpu.VMEM((BUF, 512), F32),
            pltpu.VMEM((576, 256), BF),
            pltpu.VMEM((2, 576, 256), BF),
            pltpu.VMEM((2, 2, CH, 512), BF),
            pltpu.VMEM((8, pixels), jnp.int32),
            pltpu.VMEM((1, pixels), jnp.int32),
            pltpu.VMEM((1, C), F32),
            pltpu.VMEM((1, C), F32),
            pltpu.VMEM((368, 256), BF),
            pltpu.VMEM((304, 256), BF),
            dma((11,)),
            dma((5,)),
            dma((5,)),
            dma((4,)),
            dma((2, 2)),
            dma((3,)),
            dma((3,)),
        ],
        compiler_params=pltpu.CompilerParams(
            collective_id=0, has_side_effects=True, vmem_limit_bytes=48 * 1024 * 1024
        ),
    )(
        pin(neighbours),
        pin(wet_mask.reshape(1, pixels)),
        pin(atm_gain.reshape(1, C)),
        pin(ocean_gain.reshape(1, C)),
        pin(atm_state),
        pin(ocean_state),
        *taps,
        pin(jnp.transpose(mlp_in)),
        pin(mlp_out),
    )
    return pl.pallas_call(
        write_out,
        name="write_out",
        out_shape=(out, out),
        in_specs=[vmem] * 2,
        out_specs=(hbm, hbm),
        scratch_shapes=[dma((2,))],
    )(*[pltpu.with_memory_space_constraint(x, pltpu.VMEM) for x in parts])


def solution(mesh):
    in_specs = (
        P("chan", "sector"),
        P("chan", "sector"),
        P("sector"),
        P(None, "sector"),
        P("sector"),
        P("sector"),
        P(),
        P("chan", None, None),
        P("chan", None, None),
        P("chan", None, None),
        P(),
        P(),
        P(),
    )
    out_specs = (P("chan", "sector"), P("chan", "sector"))
    return jax.shard_map(
        per_device, mesh=mesh, in_specs=in_specs, out_specs=out_specs, check_vma=False
    )
```

```python
import functools

import jax
import jax.numpy as jnp
from jax import lax
from jax.experimental import pallas as pl
from jax.experimental.pallas import tpu as pltpu
from jax.sharding import PartitionSpec as P

EPSILON = 1e-06
CH = 80
C = 160
ROWS = 32
STRIDE = 48
BUF = 1104
BC = BUF + 96
GROUP = 10
AHEAD = 2
MESH = pl.DeviceIdType.MESH
NT = (((1,), (1,)), ((), ()))
TN = (((0,), (0,)), ((), ()))
F32 = jnp.float32
BF = jnp.bfloat16


def iota(shape, dim):
    return lax.broadcasted_iota(jnp.int32, shape, dim)


def onehot(hit):
    return jnp.where(hit, 1.0, 0.0).astype(BF)


def kernel(
    nb, wet_h, ga_h, go_h, atm, oc, w1, w2, w3, mi, mo,
    out_a, out_o,
    xa, xo, wraw_0, wraw_1, wraw_2, wb, miv, mov, keys, tsel, sbuf, halo, st_a, st_b, oc_a, oc_b,
    va, bc, pbuf, nrm, fin, obuf, nbv, wet, ga, go, hsel, osel,
    lsem, psem_s, psem_r, hsem_s, hsem_r, osem_s, osem_r,
):
    wraw = (wraw_0, wraw_1, wraw_2)
    sectors = lax.axis_size("sector")
    s = lax.axis_index("sector")
    c = lax.axis_index("chan")
    pc = 1 - c
    west = lax.rem(s + sectors - 1, sectors)
    east = lax.rem(s + 1, sectors)
    partner = {"sector": s, "chan": pc}

    bar = pltpu.get_barrier_semaphore()
    pl.semaphore_signal(bar, inc=1, device_id=partner, device_id_type=MESH)
    for chip in (west, east):
        for t in range(2):
            pl.semaphore_signal(
                bar, inc=1, device_id={"sector": chip, "chan": t}, device_id_type=MESH
            )

    loads = [
        pltpu.make_async_copy(nb, nbv, lsem.at[0]),
        pltpu.make_async_copy(atm, xa.at[c], lsem.at[1]),
        pltpu.make_async_copy(oc, xo.at[c], lsem.at[2]),
        pltpu.make_async_copy(w1, wraw[0].at[c], lsem.at[3]),
        pltpu.make_async_copy(w2, wraw[1].at[c], lsem.at[4]),
        pltpu.make_async_copy(w3, wraw[2].at[c], lsem.at[5]),
        pltpu.make_async_copy(mi, miv, lsem.at[6]),
        pltpu.make_async_copy(mo, mov, lsem.at[7]),
        pltpu.make_async_copy(wet_h, wet, lsem.at[8]),
        pltpu.make_async_copy(ga_h, ga, lsem.at[9]),
        pltpu.make_async_copy(go_h, go, lsem.at[10]),
    ]
    for n in (0, 1, 2, 8):
        loads[n].start()
    loads[0].wait()

    v = nbv[:, 0:128]
    lane = iota((8, 128), 1)
    sample = lax.shift_right_logical(lane, 5) == 1
    beyond = v >= 1024
    cycle = jnp.where(beyond, v & 31, lax.shift_right_logical(v, 5))
    side = jnp.where(beyond, jnp.where(v < 1056, 1, 2), 0)
    code = jnp.max(jnp.where(sample, 4 * cycle + side, 0), axis=1, keepdims=True)
    side = code & 3
    towards = 3 * lax.shift_right_logical(code, 2) + jnp.where(side == 0, 1, 2 * side - 2)

    for b in range(8):
        v = jnp.where(towards == 3, nbv[:, 128 * b : 128 * b + 128], 0)
        v = jnp.broadcast_to(jnp.max(v, axis=0, keepdims=True), (8, 128))
        inside = v < 1024
        hop = jnp.where(inside, v - 128 * b, lane)
        col = jnp.where(inside, 1, 0)
        for _ in range(5):
            col = col + jnp.take_along_axis(col, hop, axis=1, mode="promise_in_bounds")
            hop = jnp.take_along_axis(hop, hop, axis=1, mode="promise_in_bounds")
        cyc = 4 * b + lax.shift_right_logical(lane, 5)
        keys[0, :, 128 * b : 128 * b + 128] = 32 * cyc + col
        keys[1, :, 128 * b : 128 * b + 128] = 32 * (31 - cyc) + col

    loads[1].wait()
    loads[2].wait()
    loads[8].wait()

    wet16 = jnp.broadcast_to(wet[...], (16, 1024)).astype(F32).astype(BF)

    hr = iota((256, 256), 0)
    hh = hr & 127
    far = hr >= 128
    hi = lax.shift_right_logical(hh * 205, 10)
    he = hh - 5 * hi
    key_a = jnp.where(hh < 105, 32 * hi + jnp.where(far, 27 + he, he), -1)
    key_o = jnp.where(
        (hh >= 105) & (hh < 122), 32 * (hh - 105) + jnp.where(far, 31, 0), -1
    )
    z16 = jnp.zeros((16, 256), BF)

    def picked(keys_h, key_q, lo, hi):
        parts = []
        for d in (0, 128):
            rows = slice(d + lo, d + hi)
            if lo:
                parts.append(jnp.zeros((lo, 256), BF))
            parts.append(onehot(keys_h[rows] == key_q))
            if hi < 128:
                parts.append(jnp.zeros((128 - hi, 256), BF))
        return jnp.concatenate(parts, axis=0)

    for t in range(2):
        total = jnp.zeros((96, 256), F32)
        for b in range(3):
            q = 256 * (b if t == 0 else 3 - b)
            key_q = keys[t, 0:1, q : q + 256]
            x_a = jnp.concatenate([xa[c, :, q : q + 256], z16], axis=0)
            x_o = jnp.concatenate([xo[c, :, q : q + 256], wet16[:, q : q + 256]], axis=0)
            total = total + lax.dot_general(
                x_a, picked(key_a, key_q, *((0, 48), (32, 80), (80, 112))[b]), NT, preferred_element_type=F32
            )
            total = total + lax.dot_general(
                x_o, picked(key_o, key_q, 96, 128), NT, preferred_element_type=F32
            )
        sbuf[t, 0] = total[:, :128].astype(BF)
        sbuf[t, 1] = total[:, 128:].astype(BF)

    pl.semaphore_wait(bar, 5)

    halo_copies = []
    for t in range(2):
        for d, chip in ((0, west), (1, east)):
            halo_copies.append(
                pltpu.make_async_remote_copy(
                    src_ref=sbuf.at[t, d],
                    dst_ref=halo.at[c, :, pl.ds(128 * d, 128)],
                    send_sem=hsem_s.at[2 * t + d],
                    recv_sem=hsem_r.at[d, c],
                    device_id={"sector": chip, "chan": t},
                    device_id_type=MESH,
                )
            )
    for copy in halo_copies:
        copy.start()

    def to_partner(src, dst, n):
        return pltpu.make_async_remote_copy(
            src_ref=src,
            dst_ref=dst,
            send_sem=psem_s.at[n],
            recv_sem=psem_r.at[n],
            device_id=partner,
            device_id_type=MESH,
        )

    window = pl.ds(pl.multiple_of(256 * pc, 256), 768)
    pair = [
        to_partner(atm.at[:, window], xa.at[c, :, window], 0),
        to_partner(w1, wraw[0].at[c], 1),
        to_partner(oc.at[:, window], xo.at[c, :, window], 2),
        to_partner(w2, wraw[1].at[c], 3),
        to_partner(w3, wraw[2].at[c], 4),
    ]
    for copy in pair:
        copy.start()
    for n in (3, 9, 10, 4, 5, 6, 7):
        loads[n].start()

    for b in range(3):
        q = pl.multiple_of(256 * jnp.where(c == 0, b, 3 - b), 256)
        key_q = keys[c, 0:1, pl.ds(q, 256)] - 256 * b
        tsel[b] = onehot(iota((256, 256), 0) == key_q)

    slots = [
        jnp.max(jnp.where(towards == m, iota((8, 1), 0) + 1, 0)) if m != 4 else 0
        for m in range(9)
    ]

    def prepare(n):
        wb[n, :, 480:512] = jnp.zeros((512, 32), BF)
        wb[n, 480:512, :] = jnp.zeros((32, 512), BF)
        for dyi in range(3):
            for dxi in range(3):
                k = jnp.where(c == 0, slots[3 * dyi + dxi], slots[3 * (2 - dyi) + dxi])
                w_0 = wraw[n][0, k]
                w_1 = wraw[n][1, k]
                for lanes, dst, width in (
                    (slice(0, 128), 128 * dyi, 128),
                    (slice(128, 160), 384 + 32 * dyi, 32),
                ):
                    r = 128 * dxi
                    wb[n, r : r + 80, dst : dst + width] = w_0[:, lanes]
                    wb[n, r + 80 : r + 128, dst : dst + width] = w_1[0:48, lanes]
                    r = 384 + 32 * dxi
                    wb[n, r : r + 32, dst : dst + width] = w_1[48:80, lanes]

    hl = iota((1, 256), 1)
    hh = hl & 127
    far = hl >= 128
    hi = lax.shift_right_logical(hh * 205, 10)
    he = hh - 5 * hi
    p1 = jnp.where(hh < 105, jnp.where(far, 16 * hi + 27 + he, 16 * hi + 32 + he), -1)
    p2 = jnp.where(hi == 0, p1 - 16, p1)
    r = iota((368, 256), 0)
    hsel[...] = onehot((r == p1) | (r == p2))
    oi = hh - 105
    p1 = jnp.where((oi >= 0) & (oi < 17), jnp.where(far, 16 * oi + 31, 16 * oi + 32), -1)
    p2 = jnp.where(oi == 0, p1 - 16, p1)
    r = iota((304, 256), 0)
    osel[...] = onehot((r == p1) | (r == p2))

    loads[9].wait()
    loads[10].wait()
    gain_a = ga[:, 0:128]
    gain_b = jnp.concatenate([ga[:, 128:160]] * 4, axis=1)
    ocean_a = go[:, 0:128]
    ocean_b = jnp.concatenate([go[:, 128:160]] * 4, axis=1)

    def normed(x_a, x_b, scale_a, scale_b):
        mean_sq = jnp.sum(x_a * x_a + 0.25 * (x_b * x_b), axis=1, keepdims=True) * (1.0 / C)
        inv = lax.rsqrt(mean_sq + EPSILON)
        return x_a * inv * scale_a, x_b * inv * scale_b

    def put(v, g, x_a, x_b, rows=STRIDE):
        va[v, pl.ds(g, rows)] = x_a.astype(BF)
        y = x_b.astype(BF)
        bc[v, pl.ds(g + 2 * STRIDE, rows), 0:32] = y[:, 0:32]
        bc[v, pl.ds(g + STRIDE, rows), 32:64] = y[:, 32:64]
        bc[v, pl.ds(g, rows), 64:96] = y[:, 64:96]

    for v in range(2):
        bc[v, :, 96:128] = jnp.zeros((BC, 32), BF)

    pair[0].wait_recv()
    for b in range(3):
        q = pl.multiple_of(256 * jnp.where(c == 0, b, 3 - b), 256)
        x_1 = xa[1, :, pl.ds(q, 256)]
        x_a = jnp.concatenate([xa[0, :, pl.ds(q, 256)], x_1] + [x_1[48:80]] * 3, axis=0)
        v_a = lax.dot_general(tsel[b], x_a, NT, preferred_element_type=F32)
        for il in range(8):
            i = 8 * b + il
            rows = slice(32 * il, 32 * il + 32)
            if i <= 20:
                n_a, n_b = normed(v_a[rows, :128], v_a[rows, 128:], gain_a, gain_b)
            for g in [STRIDE * (i + 1) + 16] + ([16] if i == 0 else []):
                if i <= 20:
                    st_a[g : g + 32] = v_a[rows, :128]
                    st_b[g : g + 32] = v_a[rows, 128:]
                    put(0, g, n_a, n_b, rows=32)

    loads[3].wait()
    pair[1].wait_recv()
    prepare(0)

    pair[2].wait_recv()
    for b in range(3):
        q = pl.multiple_of(256 * jnp.where(c == 0, b, 3 - b), 256)
        wet_b = jnp.broadcast_to(wet[:, pl.ds(q, 256)], (32, 256)).astype(F32).astype(BF)
        x_1 = xo[1, :, pl.ds(q, 256)]
        x_o = jnp.concatenate(
            [xo[0, :, pl.ds(q, 256)], x_1] + [x_1[48:80]] * 2 + [wet_b], axis=0
        )
        v_o = lax.dot_general(tsel[b], x_o, NT, preferred_element_type=F32)
        for il in range(8):
            i = 8 * b + il
            rows = slice(32 * il, 32 * il + 32)
            for g in [STRIDE * (i + 1) + 16] + ([16] if i == 0 else []):
                if i <= 16:
                    oc_a[g : g + 32] = v_o[rows, :128]
                    oc_b[g : g + 32] = v_o[rows, 128:]

    for n in (1, 2):
        loads[3 + n].wait()
        pair[2 + n].wait_recv()
        prepare(n)
    loads[6].wait()
    loads[7].wait()

    for d in range(2):
        for sender in range(2):
            pltpu.make_async_remote_copy(
                src_ref=sbuf.at[0, d],
                dst_ref=halo.at[sender, :, pl.ds(128 * d, 128)],
                send_sem=hsem_s.at[0],
                recv_sem=hsem_r.at[d, sender],
                device_id=partner,
                device_id_type=MESH,
            ).wait_recv()
    h_1 = halo[1, 48:80]
    h_atm = jnp.concatenate([halo[0, 0:80], halo[1, 0:80]] + [h_1] * 3, axis=0)
    h_oc = jnp.concatenate(
        [halo[0, 0:80], halo[1, 0:80]] + [h_1] * 2 + [halo[0, 80:96]] * 2, axis=0
    )
    v_a = lax.dot_general(hsel[...], h_atm, NT, preferred_element_type=F32)
    for k in range(23):
        rows = slice(16 * k, 16 * k + 16)
        g = STRIDE * k
        st_a[g : g + 16] = v_a[rows, :128]
        st_b[g : g + 16] = v_a[rows, 128:]
        put(0, g, *normed(v_a[rows, :128], v_a[rows, 128:], gain_a, gain_b), rows=16)
    v_o = lax.dot_general(osel[...], h_oc, NT, preferred_element_type=F32)
    for k in range(19):
        rows = slice(16 * k, 16 * k + 16)
        g = STRIDE * k
        oc_a[g : g + 16] = v_o[rows, :128]
        oc_b[g : g + 16] = v_o[rows, 128:]

    group = lax.shift_right_logical(iota((1, 128), 1), 5)

    def bounds(n):
        cuts = list(range(0, n, GROUP))
        if n - cuts[-1] < GROUP // 2:
            cuts.pop()
        return list(zip(cuts, cuts[1:] + [n]))

    def products(v, n, wi, lo, hi):
        a = 48 if lo == 0 else STRIDE * lo + 64
        z = STRIDE * hi + 64
        lhs = jnp.concatenate(
            [va[v, a - 48 : z - 48], va[v, a:z], va[v, a + 48 : z + 48], bc[v, a + 48 : z + 48]],
            axis=1,
        )
        pbuf[a:z] = lax.dot_general(lhs, wb[wi], NT, preferred_element_type=F32)

    def finish(v, n, epilogue, lo, hi):
        def piece(m, g, rows):
            x = pbuf[pl.ds(g - 8, rows + 16)]
            mid = slice(8, 8 + rows)
            p_b = x[:, 384:512]
            out_a = (
                x[mid, 128:256]
                + pltpu.roll(x[:, 0:128], 1, 0)[mid]
                + pltpu.roll(x[:, 256:384], rows + 15, 0)[mid]
            )
            y = jnp.where(group == 0, pltpu.roll(p_b, 1, 0)[mid], 0.0)
            y = jnp.where(group == 1, p_b[mid], y)
            y = jnp.where(group == 2, pltpu.roll(p_b, rows + 15, 0)[mid], y)
            y = y + pltpu.roll(y, 64, 1)
            epilogue(v, m, g, rows, out_a, y + pltpu.roll(y, 32, 1))

        @pl.loop(lo, hi, unroll=True)
        def _(m):
            if n > 16:
                piece(m, pl.multiple_of(STRIDE * m + STRIDE, STRIDE), STRIDE)
            else:
                piece(m, pl.multiple_of(STRIDE * m + STRIDE + 16, 16), 32)

        if hi == n and n > 16:
            piece(n, STRIDE * n + STRIDE, 16)

    def replicate(v):
        first = iota((16, 128), 0) < 8

        def mix(own, nxt):
            mask = first[:, : own.shape[1]]
            return jnp.where(mask, nxt.astype(F32), own.astype(F32)).astype(BF)

        for ref, at, lanes in (
            (va, 0, slice(0, 128)),
            (bc, 96, slice(0, 32)),
            (bc, 48, slice(32, 64)),
            (bc, 0, slice(64, 96)),
        ):
            own, nxt = ref[v, at + 48 : at + 64, lanes], ref[v, at + 96 : at + 112, lanes]
            ref[v, at : at + 16, lanes] = own
            ref[v, at + 16 : at + 48, lanes] = ref[v, at + 64 : at + 96, lanes]
            ref[v, at + 48 : at + 64, lanes] = mix(own, nxt)

    def gelu(x):
        half = 0.5 * x
        return half + half * jnp.tanh(x * (0.7978845608028654 + 0.035677408136300125 * (x * x)))

    def hidden(v, m, g, rows, o_a, o_b):
        put(v, g, gelu(o_a), gelu(o_b), rows)

    def first_state(v, m, g, rows, o_a, o_b):
        s_a = (st_a[pl.ds(g, rows)] + o_a).astype(BF).astype(F32)
        s_b = (st_b[pl.ds(g, rows)] + o_b).astype(BF).astype(F32)
        st_a[pl.ds(g, rows)] = s_a
        st_b[pl.ds(g, rows)] = s_b
        put(v, g, *normed(s_a, s_b, gain_a, gain_b), rows)

    def second_state(v, m, g, rows, o_a, o_b):
        s_a, s_b = st_a[pl.ds(g, rows)], st_b[pl.ds(g, rows)]
        t_a = (s_a + o_a).astype(BF)
        t_b = (s_b + o_b).astype(BF)
        if rows == STRIDE:
            r = pl.multiple_of(32 * m, 32)
            fin[0, pl.ds(r, 32), 0:128] = t_a[16:48]
            fin[0, pl.ds(r, 32), 128:256] = t_b[16:48]
        y_a, y_b = oc_a[pl.ds(g, rows)], oc_b[pl.ds(g, rows)]
        mask = y_b[:, 96:97]
        put(
            v,
            g,
            (y_a + 0.5 * (s_a + t_a.astype(F32))) * mask,
            (y_b + 0.5 * (s_b + t_b.astype(F32))) * mask,
            rows,
        )

    def mixed(v, m, g, rows, o_a, o_b):
        n_a, n_b = normed(
            o_a.astype(BF).astype(F32), o_b.astype(BF).astype(F32), ocean_a, ocean_b
        )
        r = pl.multiple_of(32 * m, 32)
        nrm[pl.ds(r, 32), 0:128] = n_a.astype(BF)
        nrm[pl.ds(r, 32), 128:256] = n_b.astype(BF)

    outs = []

    def send_out(n, k, src, dst):
        copy = pltpu.make_async_remote_copy(
            src_ref=src,
            dst_ref=dst,
            send_sem=osem_s.at[k],
            recv_sem=osem_r.at[k],
            device_id=partner,
            device_id_type=MESH,
        )
        copy.start()
        outs.append(copy)

    mine = pl.ds(pl.multiple_of(512 * c, 512), 512)

    def stored(n, b):
        return lax.dot_general(
            fin[n, 256 * b : 256 * b + 256][:, :160], tsel[b], TN, preferred_element_type=F32
        )

    def atmosphere_out():
        for b in range(2):
            o = pl.multiple_of(256 * jnp.where(c == 0, b, 1 - b), 256)
            t_a = stored(0, b).astype(BF)
            for k in range(2):
                obuf[0, k, :, pl.ds(o, 256)] = t_a[80 * k : 80 * k + 80]
        send_out(0, 0, obuf.at[0, pc], out_a.at[:, mine])
        out_a[:, mine] = obuf[0, c]

    def ocean_out(b):
        h = jnp.dot(
            nrm[256 * b : 256 * b + 256, :][:, :160], miv[...], preferred_element_type=F32
        )
        h = gelu(h).astype(BF)
        q = pl.multiple_of(256 * jnp.where(c == 0, b, 3 - b), 256)
        o = pl.multiple_of(256 * jnp.where(c == 0, b, 1 - b), 256)
        w_row = wet[:, pl.ds(q, 256)].astype(F32)
        here = pl.ds(pl.multiple_of(512 * c + o, 256), 256)

        def channels(k):
            u = lax.dot_general(
                mov[pl.ds(pl.multiple_of(CH * k, 16), CH)], h, NT, preferred_element_type=F32
            )
            u = jnp.dot(u.astype(BF), tsel[b], preferred_element_type=F32)
            return (xo[k, :, pl.ds(q, 256)].astype(F32) + w_row * u).astype(BF)

        obuf[1, pc, :, pl.ds(o, 256)] = channels(pc)
        send_out(1, 1 + b, obuf.at[1, pc, :, pl.ds(o, 256)], out_o.at[:, here])
        out_o[:, here] = channels(c)

    steps = []
    for k, (n, wi, epilogue) in enumerate(
        ((20, 0, hidden), (19, 1, first_state), (18, 0, hidden), (17, 1, second_state), (16, 2, mixed))
    ):
        for i, (lo, hi) in enumerate(bounds(n)):
            steps.append((k, n, wi, epilogue, i, lo, hi))
    ready = 0
    for at, (k, n, wi, epilogue, i, lo, hi) in enumerate(steps):
        while ready < min(at + AHEAD, len(steps)):
            d = steps[ready]
            if d[0] > k:
                done = steps[at - 1] if at else None
                need = min(d[6] + 2, d[1] + 1)
                if d[0] > k + 1 or done is None or done[0] < k or done[6] < min(need, n):
                    break
            products(d[0] % 2, d[1], d[2], d[5], d[6])
            ready += 1
        finish(1 - k % 2, n, epilogue, lo, hi)
        if i == 0 and k < 4:
            replicate(1 - k % 2)
        if k == 4 and i == 0:
            atmosphere_out()
        if k == 4 and hi >= 8 and lo < 8:
            ocean_out(0)
    ocean_out(1)

    for copy in halo_copies:
        copy.wait_send()
    for copy in pair:
        copy.wait_send()
    for copy in outs:
        copy.wait()


def write_out(a, o, out_a, out_o, sem):
    copies = []
    for n, (src, dst) in enumerate(((a, out_a), (o, out_o))):
        for k in range(4):
            lanes = pl.ds(256 * k, 256)
            copies.append(
                pltpu.make_async_copy(src.at[:, lanes], dst.at[:, lanes], sem.at[4 * n + k])
            )
    for copy in copies:
        copy.start()
    for copy in copies:
        copy.wait()


def per_device(
    atm_state, ocean_state, wet_mask, neighbours, west_rim, east_rim, atm_gain,
    atm_conv_in, atm_conv_out, ocean_conv, ocean_gain, mlp_in, mlp_out,
):
    vmem = pl.BlockSpec(memory_space=pltpu.VMEM)
    anym = pl.BlockSpec(memory_space=pl.ANY)
    hbm = pl.BlockSpec(memory_space=pltpu.HBM)
    pixels = atm_state.shape[1]
    pin = lambda x: pltpu.with_memory_space_constraint(x, pltpu.HBM)
    taps = [pin(jnp.transpose(w, (1, 0, 2))) for w in (atm_conv_in, atm_conv_out, ocean_conv)]
    out = jax.ShapeDtypeStruct((CH, pixels), BF)
    dma = pltpu.SemaphoreType.DMA
    parts = pl.pallas_call(
        kernel,
        name="coupled_step",
        out_shape=(out, out),
        in_specs=[anym] * 11,
        out_specs=(vmem, vmem),
        scratch_shapes=[
            pltpu.VMEM((2, CH, pixels), BF),
            pltpu.VMEM((2, CH, pixels), BF),
            pltpu.VMEM((2, 9, CH, C), BF),
            pltpu.VMEM((2, 9, CH, C), BF),
            pltpu.VMEM((2, 9, CH, C), BF),
            pltpu.VMEM((3, 512, 512), BF),
            pltpu.VMEM((C, 640), BF),
            pltpu.VMEM((C, 640), BF),
            pltpu.VMEM((2, 8, pixels), jnp.int32),
            pltpu.VMEM((3, 256, 256), BF),
            pltpu.VMEM((2, 2, 96, 128), BF),
            pltpu.VMEM((2, 96, 256), BF),
            pltpu.VMEM((BUF, 128), F32),
            pltpu.VMEM((BUF, 128), F32),
            pltpu.VMEM((BUF, 128), F32),
            pltpu.VMEM((BUF, 128), F32),
            pltpu.VMEM((2, BUF, 128), BF),
            pltpu.VMEM((2, BC, 128), BF),
            pltpu.VMEM((BUF, 512), F32),
            pltpu.VMEM((576, 256), BF),
            pltpu.VMEM((2, 576, 256), BF),
            pltpu.VMEM((2, 2, CH, 512), BF),
            pltpu.VMEM((8, pixels), jnp.int32),
            pltpu.VMEM((1, pixels), jnp.int32),
            pltpu.VMEM((1, C), F32),
            pltpu.VMEM((1, C), F32),
            pltpu.VMEM((368, 256), BF),
            pltpu.VMEM((304, 256), BF),
            dma((11,)),
            dma((5,)),
            dma((5,)),
            dma((4,)),
            dma((2, 2)),
            dma((3,)),
            dma((3,)),
        ],
        compiler_params=pltpu.CompilerParams(
            collective_id=0, has_side_effects=True, vmem_limit_bytes=48 * 1024 * 1024
        ),
    )(
        pin(neighbours),
        pin(wet_mask.reshape(1, pixels)),
        pin(atm_gain.reshape(1, C)),
        pin(ocean_gain.reshape(1, C)),
        pin(atm_state),
        pin(ocean_state),
        *taps,
        pin(jnp.transpose(mlp_in)),
        pin(mlp_out),
    )
    return pl.pallas_call(
        write_out,
        name="write_out",
        out_shape=(out, out),
        in_specs=[vmem] * 2,
        out_specs=(hbm, hbm),
        scratch_shapes=[dma((8,))],
    )(*[pltpu.with_memory_space_constraint(x, pltpu.VMEM) for x in parts])


def solution(mesh):
    in_specs = (
        P("chan", "sector"),
        P("chan", "sector"),
        P("sector"),
        P(None, "sector"),
        P("sector"),
        P("sector"),
        P(),
        P("chan", None, None),
        P("chan", None, None),
        P("chan", None, None),
        P(),
        P(),
        P(),
    )
    out_specs = (P("chan", "sector"), P("chan", "sector"))
    return jax.shard_map(
        per_device, mesh=mesh, in_specs=in_specs, out_specs=out_specs, check_vma=False
    )
```

```python
import functools

import jax
import jax.numpy as jnp
from jax import lax
from jax.experimental import pallas as pl
from jax.experimental.pallas import tpu as pltpu
from jax.sharding import PartitionSpec as P

EPSILON = 1e-06
CH = 80
C = 160
ROWS = 32
STRIDE = 48
BUF = 1104
BC = BUF + 96
GROUP = 10
AHEAD = 2
MESH = pl.DeviceIdType.MESH
NT = (((1,), (1,)), ((), ()))
TN = (((0,), (0,)), ((), ()))
F32 = jnp.float32
BF = jnp.bfloat16


def iota(shape, dim):
    return lax.broadcasted_iota(jnp.int32, shape, dim)


def onehot(hit):
    return jnp.where(hit, 1.0, 0.0).astype(BF)


def kernel(
    nb, wet_h, ga_h, go_h, atm, oc, w1, w2, w3, mi, mo,
    out_a, out_o,
    xa, xo, wraw_0, wraw_1, wraw_2, wb, miv, mov, keys, tsel, sbuf, halo, st_a, st_b, oc_a, oc_b,
    va, bc, pbuf, nrm, fin, obuf, nbv, wet, ga, go, hsel, osel,
    lsem, psem_s, psem_r, hsem_s, hsem_r, osem_s, osem_r,
):
    wraw = (wraw_0, wraw_1, wraw_2)
    sectors = lax.axis_size("sector")
    s = lax.axis_index("sector")
    c = lax.axis_index("chan")
    pc = 1 - c
    west = lax.rem(s + sectors - 1, sectors)
    east = lax.rem(s + 1, sectors)
    partner = {"sector": s, "chan": pc}

    bar = pltpu.get_barrier_semaphore()
    pl.semaphore_signal(bar, inc=1, device_id=partner, device_id_type=MESH)
    for chip in (west, east):
        for t in range(2):
            pl.semaphore_signal(
                bar, inc=1, device_id={"sector": chip, "chan": t}, device_id_type=MESH
            )

    loads = [
        pltpu.make_async_copy(nb, nbv, lsem.at[0]),
        pltpu.make_async_copy(atm, xa.at[c], lsem.at[1]),
        pltpu.make_async_copy(oc, xo.at[c], lsem.at[2]),
        pltpu.make_async_copy(w1, wraw[0].at[c], lsem.at[3]),
        pltpu.make_async_copy(w2, wraw[1].at[c], lsem.at[4]),
        pltpu.make_async_copy(w3, wraw[2].at[c], lsem.at[5]),
        pltpu.make_async_copy(mi, miv, lsem.at[6]),
        pltpu.make_async_copy(mo, mov, lsem.at[7]),
        pltpu.make_async_copy(wet_h, wet, lsem.at[8]),
        pltpu.make_async_copy(ga_h, ga, lsem.at[9]),
        pltpu.make_async_copy(go_h, go, lsem.at[10]),
    ]
    for n in (0, 1, 2, 8):
        loads[n].start()
    loads[0].wait()

    v = nbv[:, 0:128]
    lane = iota((8, 128), 1)
    sample = lax.shift_right_logical(lane, 5) == 1
    beyond = v >= 1024
    cycle = jnp.where(beyond, v & 31, lax.shift_right_logical(v, 5))
    side = jnp.where(beyond, jnp.where(v < 1056, 1, 2), 0)
    code = jnp.max(jnp.where(sample, 4 * cycle + side, 0), axis=1, keepdims=True)
    side = code & 3
    towards = 3 * lax.shift_right_logical(code, 2) + jnp.where(side == 0, 1, 2 * side - 2)

    for b in range(8):
        v = jnp.where(towards == 3, nbv[:, 128 * b : 128 * b + 128], 0)
        v = jnp.broadcast_to(jnp.max(v, axis=0, keepdims=True), (8, 128))
        inside = v < 1024
        hop = jnp.where(inside, v - 128 * b, lane)
        col = jnp.where(inside, 1, 0)
        for _ in range(5):
            col = col + jnp.take_along_axis(col, hop, axis=1, mode="promise_in_bounds")
            hop = jnp.take_along_axis(hop, hop, axis=1, mode="promise_in_bounds")
        cyc = 4 * b + lax.shift_right_logical(lane, 5)
        keys[0, :, 128 * b : 128 * b + 128] = 32 * cyc + col
        keys[1, :, 128 * b : 128 * b + 128] = 32 * (31 - cyc) + col

    loads[1].wait()
    loads[2].wait()
    loads[8].wait()

    wet16 = jnp.broadcast_to(wet[...], (16, 1024)).astype(F32).astype(BF)

    hr = iota((256, 256), 0)
    hh = hr & 127
    far = hr >= 128
    hi = lax.shift_right_logical(hh * 205, 10)
    he = hh - 5 * hi
    key_a = jnp.where(hh < 105, 32 * hi + jnp.where(far, 27 + he, he), -1)
    key_o = jnp.where(
        (hh >= 105) & (hh < 122), 32 * (hh - 105) + jnp.where(far, 31, 0), -1
    )
    z16 = jnp.zeros((16, 256), BF)

    def picked(keys_h, key_q, lo, hi):
        parts = []
        for d in (0, 128):
            rows = slice(d + lo, d + hi)
            if lo:
                parts.append(jnp.zeros((lo, 256), BF))
            parts.append(onehot(keys_h[rows] == key_q))
            if hi < 128:
                parts.append(jnp.zeros((128 - hi, 256), BF))
        return jnp.concatenate(parts, axis=0)

    for t in range(2):
        total = jnp.zeros((96, 256), F32)
        for b in range(3):
            q = 256 * (b if t == 0 else 3 - b)
            key_q = keys[t, 0:1, q : q + 256]
            x_a = jnp.concatenate([xa[c, :, q : q + 256], z16], axis=0)
            x_o = jnp.concatenate([xo[c, :, q : q + 256], wet16[:, q : q + 256]], axis=0)
            total = total + lax.dot_general(
                x_a, picked(key_a, key_q, *((0, 48), (32, 80), (80, 112))[b]), NT, preferred_element_type=F32
            )
            total = total + lax.dot_general(
                x_o, picked(key_o, key_q, 96, 128), NT, preferred_element_type=F32
            )
        sbuf[t, 0] = total[:, :128].astype(BF)
        sbuf[t, 1] = total[:, 128:].astype(BF)

    pl.semaphore_wait(bar, 5)

    halo_copies = []
    for t in range(2):
        for d, chip in ((0, west), (1, east)):
            halo_copies.append(
                pltpu.make_async_remote_copy(
                    src_ref=sbuf.at[t, d],
                    dst_ref=halo.at[c, :, pl.ds(128 * d, 128)],
                    send_sem=hsem_s.at[2 * t + d],
                    recv_sem=hsem_r.at[d, c],
                    device_id={"sector": chip, "chan": t},
                    device_id_type=MESH,
                )
            )
    for copy in halo_copies:
        copy.start()

    def to_partner(src, dst, n):
        return pltpu.make_async_remote_copy(
            src_ref=src,
            dst_ref=dst,
            send_sem=psem_s.at[n],
            recv_sem=psem_r.at[n],
            device_id=partner,
            device_id_type=MESH,
        )

    window = pl.ds(pl.multiple_of(256 * pc, 256), 768)
    pair = [
        to_partner(atm.at[:, window], xa.at[c, :, window], 0),
        to_partner(w1, wraw[0].at[c], 1),
        to_partner(oc.at[:, window], xo.at[c, :, window], 2),
        to_partner(w2, wraw[1].at[c], 3),
        to_partner(w3, wraw[2].at[c], 4),
    ]
    for copy in pair:
        copy.start()
    for n in (3, 9, 10, 4, 5, 6, 7):
        loads[n].start()

    for b in range(3):
        q = pl.multiple_of(256 * jnp.where(c == 0, b, 3 - b), 256)
        key_q = keys[c, 0:1, pl.ds(q, 256)] - 256 * b
        tsel[b] = onehot(iota((256, 256), 0) == key_q)

    slots = [
        jnp.max(jnp.where(towards == m, iota((8, 1), 0) + 1, 0)) if m != 4 else 0
        for m in range(9)
    ]

    def prepare(n):
        wb[n, :, 480:512] = jnp.zeros((512, 32), BF)
        wb[n, 480:512, :] = jnp.zeros((32, 512), BF)
        for dyi in range(3):
            for dxi in range(3):
                k = jnp.where(c == 0, slots[3 * dyi + dxi], slots[3 * (2 - dyi) + dxi])
                w_0 = wraw[n][0, k]
                w_1 = wraw[n][1, k]
                for lanes, dst, width in (
                    (slice(0, 128), 128 * dyi, 128),
                    (slice(128, 160), 384 + 32 * dyi, 32),
                ):
                    r = 128 * dxi
                    wb[n, r : r + 80, dst : dst + width] = w_0[:, lanes]
                    wb[n, r + 80 : r + 128, dst : dst + width] = w_1[0:48, lanes]
                    r = 384 + 32 * dxi
                    wb[n, r : r + 32, dst : dst + width] = w_1[48:80, lanes]

    hl = iota((1, 256), 1)
    hh = hl & 127
    far = hl >= 128
    hi = lax.shift_right_logical(hh * 205, 10)
    he = hh - 5 * hi
    p1 = jnp.where(hh < 105, jnp.where(far, 16 * hi + 27 + he, 16 * hi + 32 + he), -1)
    p2 = jnp.where(hi == 0, p1 - 16, p1)
    r = iota((368, 256), 0)
    hsel[...] = onehot((r == p1) | (r == p2))
    oi = hh - 105
    p1 = jnp.where((oi >= 0) & (oi < 17), jnp.where(far, 16 * oi + 31, 16 * oi + 32), -1)
    p2 = jnp.where(oi == 0, p1 - 16, p1)
    r = iota((304, 256), 0)
    osel[...] = onehot((r == p1) | (r == p2))

    loads[9].wait()
    loads[10].wait()
    gain_a = ga[:, 0:128]
    gain_b = jnp.concatenate([ga[:, 128:160]] * 4, axis=1)
    ocean_a = go[:, 0:128]
    ocean_b = jnp.concatenate([go[:, 128:160]] * 4, axis=1)

    def normed(x_a, x_b, scale_a, scale_b):
        mean_sq = jnp.sum(x_a * x_a + 0.25 * (x_b * x_b), axis=1, keepdims=True) * (1.0 / C)
        inv = lax.rsqrt(mean_sq + EPSILON)
        return x_a * inv * scale_a, x_b * inv * scale_b

    def put(v, g, x_a, x_b, rows=STRIDE):
        va[v, pl.ds(g, rows)] = x_a.astype(BF)
        y = x_b.astype(BF)
        bc[v, pl.ds(g + 2 * STRIDE, rows), 0:32] = y[:, 0:32]
        bc[v, pl.ds(g + STRIDE, rows), 32:64] = y[:, 32:64]
        bc[v, pl.ds(g, rows), 64:96] = y[:, 64:96]

    for v in range(2):
        bc[v, :, 96:128] = jnp.zeros((BC, 32), BF)

    pair[0].wait_recv()
    for b in range(3):
        q = pl.multiple_of(256 * jnp.where(c == 0, b, 3 - b), 256)
        x_1 = xa[1, :, pl.ds(q, 256)]
        x_a = jnp.concatenate([xa[0, :, pl.ds(q, 256)], x_1] + [x_1[48:80]] * 3, axis=0)
        v_a = lax.dot_general(tsel[b], x_a, NT, preferred_element_type=F32)
        for il in range(8):
            i = 8 * b + il
            rows = slice(32 * il, 32 * il + 32)
            if i <= 20:
                n_a, n_b = normed(v_a[rows, :128], v_a[rows, 128:], gain_a, gain_b)
            for g in [STRIDE * (i + 1) + 16] + ([16] if i == 0 else []):
                if i <= 20:
                    st_a[g : g + 32] = v_a[rows, :128]
                    st_b[g : g + 32] = v_a[rows, 128:]
                    put(0, g, n_a, n_b, rows=32)

    loads[3].wait()
    pair[1].wait_recv()
    prepare(0)

    pair[2].wait_recv()
    for b in range(3):
        q = pl.multiple_of(256 * jnp.where(c == 0, b, 3 - b), 256)
        wet_b = jnp.broadcast_to(wet[:, pl.ds(q, 256)], (32, 256)).astype(F32).astype(BF)
        x_1 = xo[1, :, pl.ds(q, 256)]
        x_o = jnp.concatenate(
            [xo[0, :, pl.ds(q, 256)], x_1] + [x_1[48:80]] * 2 + [wet_b], axis=0
        )
        v_o = lax.dot_general(tsel[b], x_o, NT, preferred_element_type=F32)
        for il in range(8):
            i = 8 * b + il
            rows = slice(32 * il, 32 * il + 32)
            for g in [STRIDE * (i + 1) + 16] + ([16] if i == 0 else []):
                if i <= 16:
                    oc_a[g : g + 32] = v_o[rows, :128]
                    oc_b[g : g + 32] = v_o[rows, 128:]

    for n in (1, 2):
        loads[3 + n].wait()
        pair[2 + n].wait_recv()
        prepare(n)
    loads[6].wait()
    loads[7].wait()

    for d in range(2):
        for sender in range(2):
            pltpu.make_async_remote_copy(
                src_ref=sbuf.at[0, d],
                dst_ref=halo.at[sender, :, pl.ds(128 * d, 128)],
                send_sem=hsem_s.at[0],
                recv_sem=hsem_r.at[d, sender],
                device_id=partner,
                device_id_type=MESH,
            ).wait_recv()
    h_1 = halo[1, 48:80]
    h_atm = jnp.concatenate([halo[0, 0:80], halo[1, 0:80]] + [h_1] * 3, axis=0)
    v_a = lax.dot_general(hsel[...], h_atm, NT, preferred_element_type=F32)
    for k in range(23):
        rows = slice(16 * k, 16 * k + 16)
        g = STRIDE * k
        st_a[g : g + 16] = v_a[rows, :128]
        st_b[g : g + 16] = v_a[rows, 128:]
        put(0, g, *normed(v_a[rows, :128], v_a[rows, 128:], gain_a, gain_b), rows=16)
    def ocean_halos():
        h_oc = jnp.concatenate(
            [halo[0, 0:80], halo[1, 0:80]] + [h_1] * 2 + [halo[0, 80:96]] * 2, axis=0
        )
        v_o = lax.dot_general(osel[...], h_oc, NT, preferred_element_type=F32)
        for k in range(19):
            rows = slice(16 * k, 16 * k + 16)
            g = STRIDE * k
            oc_a[g : g + 16] = v_o[rows, :128]
            oc_b[g : g + 16] = v_o[rows, 128:]

    group = lax.shift_right_logical(iota((1, 128), 1), 5)

    def bounds(n):
        cuts = list(range(0, n, GROUP))
        if n - cuts[-1] < GROUP // 2:
            cuts.pop()
        return list(zip(cuts, cuts[1:] + [n]))

    def products(v, n, wi, lo, hi):
        a = 48 if lo == 0 else STRIDE * lo + 64
        z = STRIDE * hi + 64
        lhs = jnp.concatenate(
            [va[v, a - 48 : z - 48], va[v, a:z], va[v, a + 48 : z + 48], bc[v, a + 48 : z + 48]],
            axis=1,
        )
        pbuf[a:z] = lax.dot_general(lhs, wb[wi], NT, preferred_element_type=F32)

    def finish(v, n, epilogue, lo, hi):
        def piece(m, g, rows):
            x = pbuf[pl.ds(g - 8, rows + 16)]
            mid = slice(8, 8 + rows)
            p_b = x[:, 384:512]
            out_a = (
                x[mid, 128:256]
                + pltpu.roll(x[:, 0:128], 1, 0)[mid]
                + pltpu.roll(x[:, 256:384], rows + 15, 0)[mid]
            )
            y = jnp.where(group == 0, pltpu.roll(p_b, 1, 0)[mid], 0.0)
            y = jnp.where(group == 1, p_b[mid], y)
            y = jnp.where(group == 2, pltpu.roll(p_b, rows + 15, 0)[mid], y)
            y = y + pltpu.roll(y, 64, 1)
            epilogue(v, m, g, rows, out_a, y + pltpu.roll(y, 32, 1))

        @pl.loop(lo, hi, unroll=True)
        def _(m):
            if n > 16:
                piece(m, pl.multiple_of(STRIDE * m + STRIDE, STRIDE), STRIDE)
            else:
                piece(m, pl.multiple_of(STRIDE * m + STRIDE + 16, 16), 32)

        if hi == n and n > 16:
            piece(n, STRIDE * n + STRIDE, 16)

    def replicate(v):
        first = iota((16, 128), 0) < 8

        def mix(own, nxt):
            mask = first[:, : own.shape[1]]
            return jnp.where(mask, nxt.astype(F32), own.astype(F32)).astype(BF)

        for ref, at, lanes in (
            (va, 0, slice(0, 128)),
            (bc, 96, slice(0, 32)),
            (bc, 48, slice(32, 64)),
            (bc, 0, slice(64, 96)),
        ):
            own, nxt = ref[v, at + 48 : at + 64, lanes], ref[v, at + 96 : at + 112, lanes]
            ref[v, at : at + 16, lanes] = own
            ref[v, at + 16 : at + 48, lanes] = ref[v, at + 64 : at + 96, lanes]
            ref[v, at + 48 : at + 64, lanes] = mix(own, nxt)

    def gelu(x):
        half = 0.5 * x
        return half + half * jnp.tanh(x * (0.7978845608028654 + 0.035677408136300125 * (x * x)))

    def hidden(v, m, g, rows, o_a, o_b):
        put(v, g, gelu(o_a), gelu(o_b), rows)

    def first_state(v, m, g, rows, o_a, o_b):
        s_a = (st_a[pl.ds(g, rows)] + o_a).astype(BF).astype(F32)
        s_b = (st_b[pl.ds(g, rows)] + o_b).astype(BF).astype(F32)
        st_a[pl.ds(g, rows)] = s_a
        st_b[pl.ds(g, rows)] = s_b
        put(v, g, *normed(s_a, s_b, gain_a, gain_b), rows)

    def second_state(v, m, g, rows, o_a, o_b):
        s_a, s_b = st_a[pl.ds(g, rows)], st_b[pl.ds(g, rows)]
        t_a = (s_a + o_a).astype(BF)
        t_b = (s_b + o_b).astype(BF)
        if rows == STRIDE:
            r = pl.multiple_of(32 * m, 32)
            fin[0, pl.ds(r, 32), 0:128] = t_a[16:48]
            fin[0, pl.ds(r, 32), 128:256] = t_b[16:48]
        y_a, y_b = oc_a[pl.ds(g, rows)], oc_b[pl.ds(g, rows)]
        mask = y_b[:, 96:97]
        put(
            v,
            g,
            (y_a + 0.5 * (s_a + t_a.astype(F32))) * mask,
            (y_b + 0.5 * (s_b + t_b.astype(F32))) * mask,
            rows,
        )

    def mixed(v, m, g, rows, o_a, o_b):
        n_a, n_b = normed(
            o_a.astype(BF).astype(F32), o_b.astype(BF).astype(F32), ocean_a, ocean_b
        )
        r = pl.multiple_of(32 * m, 32)
        nrm[pl.ds(r, 32), 0:128] = n_a.astype(BF)
        nrm[pl.ds(r, 32), 128:256] = n_b.astype(BF)

    outs = []

    def send_out(n, k, src, dst):
        copy = pltpu.make_async_remote_copy(
            src_ref=src,
            dst_ref=dst,
            send_sem=osem_s.at[k],
            recv_sem=osem_r.at[k],
            device_id=partner,
            device_id_type=MESH,
        )
        copy.start()
        outs.append(copy)

    mine = pl.ds(pl.multiple_of(512 * c, 512), 512)

    def stored(n, b):
        return lax.dot_general(
            fin[n, 256 * b : 256 * b + 256][:, :160], tsel[b], TN, preferred_element_type=F32
        )

    def atmosphere_out():
        for b in range(2):
            o = pl.multiple_of(256 * jnp.where(c == 0, b, 1 - b), 256)
            t_a = stored(0, b).astype(BF)
            for k in range(2):
                obuf[0, k, :, pl.ds(o, 256)] = t_a[80 * k : 80 * k + 80]
        send_out(0, 0, obuf.at[0, pc], out_a.at[:, mine])
        out_a[:, mine] = obuf[0, c]

    def ocean_out(b):
        h = jnp.dot(
            nrm[256 * b : 256 * b + 256, :][:, :160], miv[...], preferred_element_type=F32
        )
        h = gelu(h).astype(BF)
        q = pl.multiple_of(256 * jnp.where(c == 0, b, 3 - b), 256)
        o = pl.multiple_of(256 * jnp.where(c == 0, b, 1 - b), 256)
        w_row = wet[:, pl.ds(q, 256)].astype(F32)
        here = pl.ds(pl.multiple_of(512 * c + o, 256), 256)

        def channels(k):
            u = lax.dot_general(
                mov[pl.ds(pl.multiple_of(CH * k, 16), CH)], h, NT, preferred_element_type=F32
            )
            u = jnp.dot(u.astype(BF), tsel[b], preferred_element_type=F32)
            return (xo[k, :, pl.ds(q, 256)].astype(F32) + w_row * u).astype(BF)

        obuf[1, pc, :, pl.ds(o, 256)] = channels(pc)
        send_out(1, 1 + b, obuf.at[1, pc, :, pl.ds(o, 256)], out_o.at[:, here])
        out_o[:, here] = channels(c)

    steps = []
    for k, (n, wi, epilogue) in enumerate(
        ((20, 0, hidden), (19, 1, first_state), (18, 0, hidden), (17, 1, second_state), (16, 2, mixed))
    ):
        for i, (lo, hi) in enumerate(bounds(n)):
            steps.append((k, n, wi, epilogue, i, lo, hi))
    ready = 0
    for at, (k, n, wi, epilogue, i, lo, hi) in enumerate(steps):
        while ready < min(at + AHEAD, len(steps)):
            d = steps[ready]
            if d[0] > k:
                done = steps[at - 1] if at else None
                need = min(d[6] + 2, d[1] + 1)
                if d[0] > k + 1 or done is None or done[0] < k or done[6] < min(need, n):
                    break
            products(d[0] % 2, d[1], d[2], d[5], d[6])
            ready += 1
        finish(1 - k % 2, n, epilogue, lo, hi)
        if at == 0:
            ocean_halos()
        if i == 0 and k < 4:
            replicate(1 - k % 2)
        if k == 4 and i == 0:
            atmosphere_out()
        if k == 4 and hi >= 8 and lo < 8:
            ocean_out(0)
    ocean_out(1)

    for copy in halo_copies:
        copy.wait_send()
    for copy in pair:
        copy.wait_send()
    for copy in outs:
        copy.wait()


def write_out(a, o, out_a, out_o, sem):
    copies = []
    for n, (src, dst) in enumerate(((a, out_a), (o, out_o))):
        for k in range(4):
            lanes = pl.ds(256 * k, 256)
            copies.append(
                pltpu.make_async_copy(src.at[:, lanes], dst.at[:, lanes], sem.at[4 * n + k])
            )
    for copy in copies:
        copy.start()
    for copy in copies:
        copy.wait()


def per_device(
    atm_state, ocean_state, wet_mask, neighbours, west_rim, east_rim, atm_gain,
    atm_conv_in, atm_conv_out, ocean_conv, ocean_gain, mlp_in, mlp_out,
):
    vmem = pl.BlockSpec(memory_space=pltpu.VMEM)
    anym = pl.BlockSpec(memory_space=pl.ANY)
    hbm = pl.BlockSpec(memory_space=pltpu.HBM)
    pixels = atm_state.shape[1]
    pin = lambda x: pltpu.with_memory_space_constraint(x, pltpu.HBM)
    taps = [pin(jnp.transpose(w, (1, 0, 2))) for w in (atm_conv_in, atm_conv_out, ocean_conv)]
    out = jax.ShapeDtypeStruct((CH, pixels), BF)
    dma = pltpu.SemaphoreType.DMA
    parts = pl.pallas_call(
        kernel,
        name="coupled_step",
        out_shape=(out, out),
        in_specs=[anym] * 11,
        out_specs=(vmem, vmem),
        scratch_shapes=[
            pltpu.VMEM((2, CH, pixels), BF),
            pltpu.VMEM((2, CH, pixels), BF),
            pltpu.VMEM((2, 9, CH, C), BF),
            pltpu.VMEM((2, 9, CH, C), BF),
            pltpu.VMEM((2, 9, CH, C), BF),
            pltpu.VMEM((3, 512, 512), BF),
            pltpu.VMEM((C, 640), BF),
            pltpu.VMEM((C, 640), BF),
            pltpu.VMEM((2, 8, pixels), jnp.int32),
            pltpu.VMEM((3, 256, 256), BF),
            pltpu.VMEM((2, 2, 96, 128), BF),
            pltpu.VMEM((2, 96, 256), BF),
            pltpu.VMEM((BUF, 128), F32),
            pltpu.VMEM((BUF, 128), F32),
            pltpu.VMEM((BUF, 128), F32),
            pltpu.VMEM((BUF, 128), F32),
            pltpu.VMEM((2, BUF, 128), BF),
            pltpu.VMEM((2, BC, 128), BF),
            pltpu.VMEM((BUF, 512), F32),
            pltpu.VMEM((576, 256), BF),
            pltpu.VMEM((2, 576, 256), BF),
            pltpu.VMEM((2, 2, CH, 512), BF),
            pltpu.VMEM((8, pixels), jnp.int32),
            pltpu.VMEM((1, pixels), jnp.int32),
            pltpu.VMEM((1, C), F32),
            pltpu.VMEM((1, C), F32),
            pltpu.VMEM((368, 256), BF),
            pltpu.VMEM((304, 256), BF),
            dma((11,)),
            dma((5,)),
            dma((5,)),
            dma((4,)),
            dma((2, 2)),
            dma((3,)),
            dma((3,)),
        ],
        compiler_params=pltpu.CompilerParams(
            collective_id=0, has_side_effects=True, vmem_limit_bytes=48 * 1024 * 1024
        ),
    )(
        pin(neighbours),
        pin(wet_mask.reshape(1, pixels)),
        pin(atm_gain.reshape(1, C)),
        pin(ocean_gain.reshape(1, C)),
        pin(atm_state),
        pin(ocean_state),
        *taps,
        pin(jnp.transpose(mlp_in)),
        pin(mlp_out),
    )
    return pl.pallas_call(
        write_out,
        name="write_out",
        out_shape=(out, out),
        in_specs=[vmem] * 2,
        out_specs=(hbm, hbm),
        scratch_shapes=[dma((8,))],
    )(*[pltpu.with_memory_space_constraint(x, pltpu.VMEM) for x in parts])


def solution(mesh):
    in_specs = (
        P("chan", "sector"),
        P("chan", "sector"),
        P("sector"),
        P(None, "sector"),
        P("sector"),
        P("sector"),
        P(),
        P("chan", None, None),
        P("chan", None, None),
        P("chan", None, None),
        P(),
        P(),
        P(),
    )
    out_specs = (P("chan", "sector"), P("chan", "sector"))
    return jax.shard_map(
        per_device, mesh=mesh, in_specs=in_specs, out_specs=out_specs, check_vma=False
    )
```
